256 devices in a mesh: site: 8 (over y, core), sector: 32 (over z, x).
Axes of the slice: x: 4, y: 4, z: 8, core: 2. Of those that a mesh axis runs over, the one named last changes fastest.
Arguments:
- env_in: bfloat16 [256, 20, 1024], P('sector'), as said below
- mpo_terms: bfloat16 [4, 20, 20], replicated, may hold values from -1.25 to 1.25
- site_tensors: bfloat16 [8, 256, 4, 1024], P('site', 'sector'), may hold values from -0.75 to 0.75
- route_owner: int32 [8, 256, 4, 1], P('site'), may hold values from 0 to 31; in each aligned block of 32 rows (0 to 31, 32 to 63, ..., all dimensions but the last counted through in order) at most 2 rows name the same one
- route_sector: int32 [8, 256, 4], P('site'), may hold values from 0 to 7
- live_block_extent: int32 [256], P('sector'), may hold values from 8 to 32, as said below
- psi: bfloat16 [8, 256, 1024], P('site', 'sector'), may hold values from -6 to 6
- right_env: bfloat16 [8, 256, 20, 1024], P('site', 'sector'), as said below
Outputs:
- ground: float32 [8, 256, 1024], P('site', 'sector')
- site_energy: float32 [8], P('site')
The draws below stay inside these ranges and needn't reach their ends.
Inputs may be any that keep to these rules, and one draw needn't show every extreme that they name: `route_owner`: among the rows of one device at one site (8 sectors times 4 states) no owner is named more than 2 times, and some device's rows name one owner exactly 2 times. `live_block_extent`: some sector block is full in every draw. `env_in`: each block is symmetric in its two block indices for every bond index. `right_env`: each block is symmetric in its two block indices for every bond index.
All inputs are finite; a program needn't handle non-finite values.
Results may differ from the reference program's by a relative error of at most 0.03.
Values may be sent and summed in bfloat16 or wider, within the bound.
No kernel may reach another device: no remote copies, remote signals or barrier semaphores. Data moves between devices by JAX's collectives and lax.ppermute only.
A program may use at most 64 MiB of HBM per device.

```python
import math
import jax
import jax.numpy as jnp
import numpy as np
from jax import lax

B = 32
W_BOND = 20
SEC_DEV = 8
PHYS = 4
DAV_ITERS = 2
CAP = 2
S = 256
SITES = 8
N_SECTOR = 32


def draw_env_in(key, part):
    raw_values = jax.random.normal(key, (S, W_BOND, B, B), jnp.float32)
    symmetric = (raw_values + jnp.swapaxes(raw_values, 2, 3)) * (0.7071 / math.sqrt(B))
    return symmetric.reshape(S, W_BOND, B * B).astype(jnp.bfloat16)


def draw_right_env(key, part):
    first_key, second_key = jax.random.split(jax.random.fold_in(key, 7))
    raw_values = jax.random.normal(first_key, (SITES, S, W_BOND, B, B), jnp.float32)
    diagonal = jnp.exp(jax.random.uniform(second_key, (SITES, S, B), jnp.float32, math.log(0.5), math.log(2.0)))
    symmetric = (raw_values + jnp.swapaxes(raw_values, 3, 4)) * (0.35 / math.sqrt(B * W_BOND))
    identity = jnp.eye(B, dtype=jnp.float32)
    first_bond = (jnp.arange(W_BOND) == 0).astype(jnp.float32)
    plane = first_bond[:, None, None] * identity[None, :, :]
    whole = symmetric + diagonal[:, :, None, :, None] * plane[None, None]
    return whole.reshape(SITES, S, W_BOND, B * B).astype(jnp.bfloat16)


def draw_live_block_extent(key, part):
    first_key, second_key = jax.random.split(jax.random.fold_in(key, 11))
    sizes = jax.random.randint(first_key, (S,), B // 4, B + 1)
    chosen = jax.random.randint(second_key, (), 0, S)
    return jnp.where(jnp.arange(S) == chosen, B, sizes).astype(jnp.int32)


def place_ends(entries, own_key, least, largest):
    longest = entries.shape.index(max(entries.shape))
    spots = []
    for shift in (0, 1):
        where = [jax.random.randint(jax.random.fold_in(own_key, axis), (), 0, length) for axis, length in enumerate(entries.shape)]
        where[longest] = (where[longest] + shift) % entries.shape[longest]
        spots.append(tuple(where))
    return entries.at[spots[0]].set(least).at[spots[1]].set(largest)


def steps_of(stream_key, dims, pieces, low, high):
    def one(position, blocks):
        steps = jax.random.uniform(jax.random.fold_in(jax.random.fold_in(stream_key, 6), position), (blocks,), jnp.float32, low / len(pieces), high / len(pieces))
        return jnp.repeat(jnp.exp(steps), dims[position] // blocks).reshape((-1,) + (1,) * (len(dims) - position - 1))

    gain = one(*pieces[0])
    for cut in pieces[1:]:
        gain = gain * one(*cut)
    return gain


def shared_out(own_key, own, number, rows, number_of, top, most, skew):
    sequence = jax.random.permutation(own_key, number_of)
    crowded, ordinary = load_shares(number_of, rows * top, most, skew, True), load_shares(number_of, rows * top, most, skew, False)
    places = jnp.arange(number_of)

    def named(sizes, offset_by):
        used = int((sizes > 0).sum())
        fixed = max(1, used // 4)
        shifted = fixed + (places - fixed + offset_by * (used - fixed)) % max(1, number_of - fixed)
        return jnp.zeros((number_of,), jnp.int32).at[sequence[jnp.where(places < fixed, places, shifted)]].set(jnp.asarray(sizes, jnp.int32))

    sizes = jnp.where(number % 4 == 0, named(crowded, number // 4), named(ordinary, number - number // 4 - 1))
    mixed = jax.random.permutation(jax.random.fold_in(own, 3), number_of)
    source_of, sink = mixed[0:number_of // 2 * 2:2], mixed[1:number_of // 2 * 2:2]
    margin = jnp.minimum(sizes[source_of] - 1, most - sizes[sink]) // 2
    margin = jnp.where((source_of == sequence[0]) | (sink == sequence[0]) | (sizes[sink] == 0), 0, jnp.maximum(margin, 0))
    shifted = jax.random.randint(jax.random.fold_in(own, 4), (number_of // 2,), 0, 1 << 20) % (margin + 1)
    sizes = sizes.at[source_of].add(-shifted).at[sink].add(shifted)
    labels = jnp.searchsorted(jnp.cumsum(sizes), jnp.arange(rows * top), side="right").astype(jnp.int32)
    listing = labels.reshape(top, rows).T
    listing = listing[jax.random.permutation(jax.random.fold_in(own, 1), rows)]
    offset_by = jax.random.randint(jax.random.fold_in(own, 2), (rows, 1), 0, top)
    return jnp.take_along_axis(listing, (jnp.arange(top)[None, :] + offset_by) % top, axis=1)


def load_shares(amount, total, reach, slope, full):
    loads = [(1 << 20) // math.isqrt(grade ** slope) + 1 for grade in range(1, amount + 1)]
    largest = reach if full else min(reach, max(-(-total // amount), total * loads[0] // sum(loads)))
    least = 1 if total - largest >= amount - 1 else 0
    given, spare = [largest] + [least] * (amount - 1), total - largest - least * (amount - 1)
    while spare > 0:
        movable = [i for i in range(1, amount) if given[i] < largest] or [i for i in range(1, amount) if given[i] < reach]
        whole, budget = sum([loads[i] for i in movable]), spare
        for i in movable:
            extra = min(reach - given[i], max(1, budget * loads[i] // whole), spare)
            given[i] = given[i] + extra
            spare = spare - extra
    return np.array(given)


def centred(stream_key, shape, width, reach, pieces=(), kind=jnp.bfloat16):
    drawn = jax.random.normal(stream_key, shape, jnp.float32) * width
    if len(pieces) > 0:
        drawn = steps_of(stream_key, shape, pieces, -0.22, 0.18) * drawn
    return jnp.clip(drawn, min=-reach, max=reach).astype(kind)


def setup_inputs(seed: int = 0) -> dict:
    key_of = jax.random.split(jax.random.key(seed), 9)
    env_in = draw_env_in(jax.random.fold_in(key_of[8], 71), 0)
    mpo_terms = centred(key_of[1], (PHYS, W_BOND, W_BOND), W_BOND ** -0.5, 1.25)
    site_tensors = centred(key_of[2], (SITES, S, PHYS, B * B), (2 * B) ** -0.5, 0.75, ((0, 8), (1, 32)))
    route_owner_keys = jax.random.split(jax.random.fold_in(key_of[3], 1), SITES * S * PHYS // (SEC_DEV * PHYS))
    route_owner_turns = jax.random.permutation(jax.random.fold_in(key_of[3], 3), SITES * S * PHYS // (SEC_DEV * PHYS))
    route_owner = jax.vmap(lambda own, number: shared_out(jax.random.fold_in(key_of[3], 2), own, number, SEC_DEV * PHYS, N_SECTOR, 1, CAP, 2))(route_owner_keys, route_owner_turns).reshape((SITES, S, PHYS, 1))
    route_sector = place_ends(jax.random.randint(key_of[4], (SITES, S, PHYS), 0, SEC_DEV), jax.random.fold_in(key_of[4], 1), 0, SEC_DEV - 1).astype(jnp.int32)
    live_block_extent = draw_live_block_extent(jax.random.fold_in(key_of[8], 71), 0)
    psi = centred(key_of[6], (SITES, S, B * B), 1.0, 6.0, ((0, 8), (1, 32)))
    right_env = draw_right_env(jax.random.fold_in(key_of[8], 71), 0)
    return dict(env_in=env_in, mpo_terms=mpo_terms, site_tensors=site_tensors, route_owner=route_owner, route_sector=route_sector, live_block_extent=live_block_extent, psi=psi, right_env=right_env)


epsilon = 1e-06

def spread(values):
    return values[:, None, None, None]

def reference(env_in, mpo_terms, site_tensors, route_owner, route_sector, live_block_extent, psi, right_env):
    count_all = S * B * B
    target = (route_owner[..., 0] * SEC_DEV + route_sector).astype(jnp.int32)
    mpo_full = mpo_terms.astype(jnp.float32)

    def chain_step(left_env, inputs):
        tensors, goals = inputs
        env_blocks = left_env.reshape(S, W_BOND, B, B).astype(jnp.float32)
        tensor_blocks = tensors.reshape(S, PHYS, B, B).astype(jnp.float32)
        mixed = jnp.einsum('swab,pwv->spvab', env_blocks, mpo_full).astype(jnp.bfloat16)
        halfway = jnp.einsum('spvab,spbc->spvac', mixed.astype(jnp.float32), tensor_blocks).astype(jnp.bfloat16)
        blocks = jnp.einsum('spad,spvac->spvdc', tensor_blocks, halfway.astype(jnp.float32)).astype(jnp.bfloat16)
        summed = jax.ops.segment_sum(blocks.astype(jnp.float32).reshape(S * PHYS, W_BOND, B * B), goals.reshape(S * PHYS), num_segments=S)
        return (summed.astype(jnp.bfloat16), left_env)
    last_env, left_environments = lax.scan(chain_step, env_in, (site_tensors, target))
    site_positions = jnp.arange(B, dtype=jnp.int32)
    live_flags = site_positions[None, :] < live_block_extent[:, None]
    sector_block_mask = (live_flags[:, :, None] & live_flags[:, None, :]).astype(jnp.float32)
    left_full = left_environments.astype(jnp.float32).reshape(SITES, S, W_BOND, B, B)
    right_full = right_env.astype(jnp.float32).reshape(SITES, S, W_BOND, B, B)

    def operate(field):
        product = jnp.einsum('nswab,nsbc->nswac', left_full, field, precision=lax.Precision.HIGHEST)
        product = jnp.einsum('nswac,nswcd->nsad', product, right_full, precision=lax.Precision.HIGHEST)
        return product * sector_block_mask

    def inner_product(former, latter):
        return lax.optimization_barrier(jnp.sum(former * latter, axis=(1, 2, 3))) / count_all
    left_diag = jnp.diagonal(left_full, axis1=3, axis2=4)
    right_diag = jnp.diagonal(right_full, axis1=3, axis2=4)
    precond = jnp.einsum('nswa,nswb->nsab', left_diag, right_diag, precision=lax.Precision.HIGHEST)
    start = psi.astype(jnp.float32).reshape(SITES, S, B, B) * sector_block_mask
    trial_vector = start / spread(jnp.sqrt(inner_product(start, start) + epsilon))
    image = operate(trial_vector)
    energy = inner_product(trial_vector, image)
    for sweep_index in range(DAV_ITERS):
        residual_vector = image - spread(energy) * trial_vector
        correction = residual_vector / jnp.maximum(precond - spread(energy), 1.0)
        correlation = inner_product(trial_vector, correction)
        orthogonal = correction - spread(correlation) * trial_vector
        direction = orthogonal / spread(jnp.sqrt(inner_product(orthogonal, orthogonal) + epsilon))
        applied = operate(direction)
        coupling = inner_product(direction, image)
        curvature = inner_product(direction, applied)
        angle = 0.5 * jnp.arctan2(-2.0 * coupling, curvature - energy)
        trial_vector = spread(jnp.cos(angle)) * trial_vector + spread(jnp.sin(angle)) * direction
        image = spread(jnp.cos(angle)) * image + spread(jnp.sin(angle)) * applied
        energy = inner_product(trial_vector, image)
    return (trial_vector.reshape(SITES, S, B * B), energy)
```

```python
import jax
import jax.numpy as jnp
from jax import lax
from jax.sharding import PartitionSpec as P

B = 32
W_BOND = 20
PHYS = 4
DAV_ITERS = 2


epsilon = 1e-06


def from_behind(block, axis, distance):
    devices = range(lax.axis_size(axis))
    route = [(i - distance, i) for i in devices if i - distance in devices]
    return lax.ppermute(block, axis, route)


def spread(values):
    return values[:, None, None, None]


def contract(left_env, mpo_terms, tensors):
    sec_count = left_env.shape[0]
    env_blocks = left_env.reshape(sec_count, W_BOND, B, B)
    tensor_blocks = tensors.reshape(sec_count, PHYS, B, B)
    mixed = jnp.einsum(
        "swab,pwv->spvab", env_blocks, mpo_terms, preferred_element_type=jnp.float32
    ).astype(jnp.bfloat16)
    halfway = jnp.einsum(
        "spvab,spbc->spvac", mixed, tensor_blocks, preferred_element_type=jnp.float32
    ).astype(jnp.bfloat16)
    return jnp.einsum(
        "spad,spvac->spvdc", tensor_blocks, halfway, preferred_element_type=jnp.float32
    ).astype(jnp.bfloat16)


def slot_ranks(owner_grid):
    site_positions = jnp.arange(owner_grid.shape[1])
    earlier = site_positions[None, :] < site_positions[:, None]
    same_owner = owner_grid[:, :, None] == owner_grid[:, None, :]
    return jnp.sum(jnp.where(same_owner & earlier[None], 1, 0), axis=2).astype(jnp.int32)


def local_sum(former, latter):
    return jnp.sum(former * latter, axis=(1, 2, 3))


def sector_sums(parts):
    n_sector = lax.axis_size("sector")
    row = jnp.pad(jnp.stack(parts), (0, 128 - len(parts)))
    sent = jnp.broadcast_to(row[None, None, :], (n_sector, 1, 128))
    got = lax.all_to_all(sent, "sector", split_axis=0, concat_axis=0, tiled=True)
    total = jnp.sum(got, axis=(0, 1))
    return [total[i] for i in range(len(parts))]


def local(
    env_in, mpo_terms, site_tensors, route_owner, route_sector, live_block_extent, psi, right_env
):
    n_sector = lax.axis_size("sector")
    n_site = lax.axis_size("site")
    member = lax.axis_index("sector")
    segment_index = lax.axis_index("site")
    sites_dev = site_tensors.shape[0]
    sec_dev = site_tensors.shape[1]
    state_count = site_tensors.shape[2]
    sector_total = sec_dev * n_sector
    row_count = sec_dev * state_count
    capacity = max(2, 2 * row_count // n_sector)
    owners = route_owner[..., 0]
    env_shape = (sec_dev, W_BOND, B * B)

    def route(blocks, site_local):
        flat_blocks = blocks.reshape(row_count, W_BOND * B * B)
        owner_grid = owners[site_local].reshape(n_sector, row_count)
        worker_grid = route_sector[site_local].reshape(n_sector, row_count)
        rank_grid = slot_ranks(owner_grid)
        own_row = lax.dynamic_index_in_dim(owner_grid, member, 0, keepdims=False)
        rank_row = lax.dynamic_index_in_dim(rank_grid, member, 0, keepdims=False)
        send_pick = (
            (own_row[None, None, :] == jnp.arange(n_sector)[:, None, None])
            & (rank_row[None, None, :] == jnp.arange(capacity)[None, :, None])
        ).astype(jnp.bfloat16)
        outbox = jnp.einsum(
            "ocr,rk->ock", send_pick, flat_blocks, preferred_element_type=jnp.float32
        ).astype(jnp.bfloat16)
        inbox = lax.all_to_all(outbox, "sector", split_axis=0, concat_axis=0, tiled=True)
        taken = (owner_grid == member)[None] & (
            worker_grid[None] == jnp.arange(sec_dev)[:, None, None]
        )
        slot_match = rank_grid[None, :, None, :] == jnp.arange(capacity)[None, None, :, None]
        receive_pick = jnp.sum(
            jnp.where(taken[:, :, None, :] & slot_match, 1.0, 0.0), axis=3
        ).astype(jnp.bfloat16)
        summed = jnp.einsum(
            "tpc,pck->tk", receive_pick, inbox, preferred_element_type=jnp.float32
        ).astype(jnp.bfloat16)
        return summed.reshape(env_shape)

    def segment(left_env):
        entering = [left_env]
        left_env = route(contract(left_env, mpo_terms, site_tensors[0]), 0)
        return (left_env, jnp.stack(entering))

    first_env = jnp.where(segment_index == 0, env_in, jnp.zeros_like(env_in))

    def advance(turn, current):
        leaving, unused = segment(current)
        moved = from_behind(leaving, "site", 1)
        return jnp.where(segment_index == 0, env_in, moved)

    current_env = lax.fori_loop(0, n_site - 1, advance, first_env)
    unused_env, left_environments = segment(current_env)
    site_positions = jnp.arange(B, dtype=jnp.int32)
    live_flags = site_positions[None, :] < live_block_extent[:, None]
    sector_block_mask = (live_flags[:, :, None] & live_flags[:, None, :]).astype(jnp.float32)
    left_full = left_environments.astype(jnp.float32).reshape(sites_dev, sec_dev, W_BOND, B, B)
    right_full = right_env.astype(jnp.float32).reshape(sites_dev, sec_dev, W_BOND, B, B)
    count_all = float(sector_total * B * B)

    def operate(field):
        product = jnp.einsum("nswab,nsbc->nswac", left_full, field, precision=lax.Precision.HIGHEST)
        product = jnp.einsum(
            "nswac,nswcd->nsad", product, right_full, precision=lax.Precision.HIGHEST
        )
        return product * sector_block_mask

    left_diag = jnp.diagonal(left_full, axis1=3, axis2=4)
    right_diag = jnp.diagonal(right_full, axis1=3, axis2=4)
    precond = jnp.einsum("nswa,nswb->nsab", left_diag, right_diag, precision=lax.Precision.HIGHEST)
    start = psi.astype(jnp.float32).reshape(sites_dev, sec_dev, B, B) * sector_block_mask
    def dot(former, latter):
        return jnp.sum(former * latter)

    raw_image = operate(start)
    start_norm, raw_energy = sector_sums([dot(start, start), dot(start, raw_image)])
    start_norm, raw_energy = start_norm / count_all, raw_energy / count_all
    scale = 1.0 / jnp.sqrt(start_norm + epsilon)
    trial_vector = start * scale
    image = raw_image * scale
    energy = raw_energy * scale * scale
    for sweep_index in range(DAV_ITERS):
        residual_vector = image - energy * trial_vector
        correction = residual_vector / jnp.maximum(precond - energy, 1.0)
        lifted = operate(correction)
        sums = sector_sums(
            [
                dot(trial_vector, correction),
                dot(correction, correction),
                dot(trial_vector, trial_vector),
                dot(correction, image),
                dot(correction, lifted),
                dot(trial_vector, lifted),
                dot(trial_vector, image),
            ]
        )
        vc, cc, vv, ci, cl, vl, vi = [entry / count_all for entry in sums]
        length_sq = jnp.maximum(cc - 2.0 * vc * vc + vc * vc * vv, 0.0)
        inverse = 1.0 / jnp.sqrt(length_sq + epsilon)
        direction = (correction - vc * trial_vector) * inverse
        applied = (lifted - vc * image) * inverse
        coupling = (ci - vc * vi) * inverse
        curvature = (cl - vc * vl - vc * ci + vc * vc * vi) * inverse * inverse
        crossed = (vl - vc * vi) * inverse
        angle = 0.5 * jnp.arctan2(-2.0 * coupling, curvature - energy)
        cosine, sine = jnp.cos(angle), jnp.sin(angle)
        trial_vector = cosine * trial_vector + sine * direction
        image = cosine * image + sine * applied
        energy = cosine * cosine * vi + cosine * sine * (crossed + coupling) + sine * sine * curvature
    energy = energy.reshape(1)
    return (trial_vector.reshape(sites_dev, sec_dev, B * B), energy)


def solution(mesh):
    in_specs = (
        P("sector", None, None),
        P(),
        P("site", "sector", None, None),
        P("site", None, None, None),
        P("site", None, None),
        P("sector"),
        P("site", "sector", None),
        P("site", "sector", None, None),
    )
    out_specs = (P("site", "sector", None), P("site"))
    return jax.shard_map(local, mesh=mesh, in_specs=in_specs, out_specs=out_specs, check_vma=False)
```

```python
import functools

import jax
import jax.numpy as jnp
from jax import lax
from jax.experimental import pallas as pl
from jax.experimental.pallas import tpu as pltpu
from jax.sharding import PartitionSpec as P

B = 32
W_BOND = 20
HALF = W_BOND // 2
PHYS = 4
SEC = 8
DAV_ITERS = 2
CAP = 2
N_SITE = 8
N_SECTOR = 32
SLOTS = N_SECTOR * CAP
ROWS = SEC * PHYS
LANES = SEC * B
PACK = 56
COUNT_ALL = float(N_SECTOR * SEC * B * B)
epsilon = 1e-06
bf16, f32 = jnp.bfloat16, jnp.float32
BOTH = ("site", "sector")


def flat(high, low_core, group, rest):
    return (high * 2 + low_core) * N_SECTOR + group * 8 + rest


def every_device():
    return [(y, c, g, r) for y in range(4) for c in range(2) for g in range(4) for r in range(8)]


def turn(block, step):
    pairs = [(flat(y, c, g, r), flat(g, c, (y + step) % 4, r)) for y, c, g, r in every_device()]
    return lax.ppermute(block, BOTH, pairs)


def exchange(block):
    groups = [
        [flat(y, c, g, r) for y in range(4) for r in range(8)] for g in range(4) for c in range(2)
    ]
    return lax.all_to_all(block, BOTH, split_axis=0, concat_axis=0, tiled=True, axis_index_groups=groups)


def other_core(block):
    return lax.ppermute(block, "site", [(i, i ^ 1) for i in range(N_SITE)])


def iota(shape, axis):
    return lax.broadcasted_iota(jnp.int32, shape, axis)


def block_mask(rows, lanes):
    same = (iota((rows, lanes), 0) // B) == (iota((rows, lanes), 1) // B)
    return jnp.where(same, 1.0, 0.0).astype(bf16)


def spread_blocks(field, mask):
    return jnp.concatenate([field] * SEC, axis=0) * mask


def column_block():
    return (iota((8, 128), 1) % B) // 8


def half_to_tiles(square):
    cb = column_block()

    def chosen(step, tile):
        parts = [tile[8 * d : 8 * d + 8, :] for d in range(4)]
        picked = parts[(3 + step) % 4]
        for d in (2, 1, 0):
            picked = jnp.where(cb == d, parts[(d + step) % 4], picked)
        return picked

    lane = iota((8, 128), 1)
    s = [[chosen(step, tile) for tile in square] for step in range(3)]
    return [
        s[0][0],
        s[0][1],
        s[1][0],
        s[1][1],
        jnp.where(lane < 64, s[0][2], pltpu.roll(s[1][2], 64, 1)),
        jnp.where(cb < 2, s[2][0], pltpu.roll(s[2][1], 16, 1)),
        s[2][2],
    ]


def tiles_to_half(tiles):
    cb = column_block()
    diag = [tiles[0], tiles[1], tiles[4]]
    near = [tiles[2], tiles[3], pltpu.roll(tiles[4], 64, 1)]
    far = [tiles[5], pltpu.roll(tiles[5], 112, 1), tiles[6]]
    square = []
    for tile in range(3):
        rows = []
        for d in range(4):
            rows.append(
                jnp.where(
                    cb == d, diag[tile], jnp.where(cb == (d - 1) % 4, near[tile], far[tile])
                )
            )
        square.append(jnp.concatenate(rows, axis=0))
    return square


def moved(sources, shifts):
    quarter = iota((B, 128), 1) // B
    total = None
    for k, (source, shift) in enumerate(zip(sources, shifts)):
        shift = shift % 128
        piece = pltpu.roll(source, shift, 1) if shift else source
        total = piece if total is None else jnp.where(quarter == k, piece, total)
    return total


def write_tall(core, mine_ref, other_ref, wide_ref, tall_ref):
    first = jnp.full((PACK, 128), core, jnp.int32) == 0
    ab = iota((B, LANES), 0) // 8
    bb = (iota((B, LANES), 1) % B) // 8
    gap = (ab - bb) & 3
    valid = (gap < 2) | ((gap == 2) & (bb < 2))
    for half in range(2):
        squares = []
        for t in range(SEC):
            mine, other = mine_ref[t].astype(f32), other_ref[t].astype(f32)
            whole = jnp.where(first, mine, other) if half == 0 else jnp.where(first, other, mine)
            square = tiles_to_half([whole[8 * i : 8 * i + 8, :] for i in range(7)])
            squares.append(square)
            for tile in range(3):
                wide_ref[t * B : (t + 1) * B, tile * 128 : (tile + 1) * 128] = square[tile]
        turned = jnp.transpose(wide_ref[...])
        for v in range(HALF):
            tile, offset = v // 4, (v % 4) * B
            straight = jnp.concatenate(
                [
                    moved(
                        [squares[4 * q + k][tile] for k in range(4)],
                        [k * B - offset for k in range(4)],
                    )
                    for q in range(2)
                ],
                axis=1,
            )
            w = half * HALF + v
            row = jnp.where(valid, straight, turned[v * B : (v + 1) * B, :])
            tall_ref[w * B : (w + 1) * B, :] = row.astype(bf16)


def contract_rows(i, info_ref, mpo_ref, tensor_ref, far_tensor_ref, tall, out_ref):
    place = info_ref[N_SITE, i]
    near_core = jnp.full((B, LANES), place, jnp.int32) < 4
    turned = place & 3
    mask = block_mask(LANES, LANES)
    same_row = iota((B, W_BOND * B), 0) == (iota((B, W_BOND * B), 1) % B)
    row_mask = jnp.where(same_row, 1.0, 0.0).astype(bf16)
    for p in range(PHYS):
        mixer = jnp.concatenate(
            [
                jnp.broadcast_to(mpo_ref[p * HALF + v : p * HALF + v + 1, :], (B, W_BOND * B)) * row_mask
                for v in range(HALF)
            ],
            axis=0,
        )
        mixed = jnp.dot(mixer, tall, preferred_element_type=f32).astype(bf16)
        rows = slice(p * B, (p + 1) * B)
        tensor = jnp.where(
            near_core, tensor_ref[turned, rows, :].astype(f32), far_tensor_ref[turned, rows, :].astype(f32)
        )
        right = spread_blocks(tensor.astype(bf16), mask)
        halfway = jnp.dot(mixed, right, preferred_element_type=f32)
        wide = []
        for s in range(SEC):
            source, offset = (s // 4) * 128, (s % 4) * B
            tiles = []
            for tile in range(3):
                bonds = [v for v in range(4 * tile, 4 * tile + 4) if v < HALF]
                tiles.append(
                    moved(
                        [halfway[v * B : (v + 1) * B, source : source + 128] for v in bonds],
                        [(v % 4) * B - offset for v in bonds],
                    )
                )
            wide.append(jnp.concatenate(tiles, axis=1))
        wide = jnp.concatenate(wide, axis=0).astype(bf16)
        blocks = lax.dot_general(right, wide, (((0,), (0,)), ((), ())), preferred_element_type=f32)
        for s in range(SEC):
            tiles = half_to_tiles(
                [blocks[s * B : (s + 1) * B, tile * 128 : (tile + 1) * 128] for tile in range(3)]
            )
            out_ref[info_ref[place, s * PHYS + p]] = jnp.concatenate(tiles, axis=0).astype(bf16)


def first_kernel(info_ref, mpo_ref, tensor_ref, far_tensor_ref, tall_ref, out_ref):
    contract_rows(0, info_ref, mpo_ref, tensor_ref, far_tensor_ref, tall_ref[...], out_ref)


def expand_kernel(i, info_ref, mpo_ref, tensor_ref, far_tensor_ref, mine_ref, other_ref, *rest):
    out_ref, tall_ref, wide_ref = rest
    write_tall(info_ref[N_SITE, N_SITE], mine_ref, other_ref, wide_ref, tall_ref)
    contract_rows(i, info_ref, mpo_ref, tensor_ref, far_tensor_ref, tall_ref[...], out_ref)


def collect_kernel(i, info_ref, inbox_ref, out_ref, total_ref):
    place = info_ref[N_SITE, i]
    total_ref[...] = jnp.zeros_like(total_ref)
    for q in range(SLOTS):
        t = info_ref[place, ROWS + q]

        @pl.when(t > 0)
        def _():
            total_ref[t - 1] += inbox_ref[q].astype(f32)

    out_ref[...] = total_ref[...].astype(bf16)


VMEM = pl.BlockSpec(memory_space=pltpu.VMEM)
SMEM = pl.BlockSpec(memory_space=pltpu.SMEM)
PARAMS = pltpu.CompilerParams(vmem_limit_bytes=48 << 20)


def call(kernel, ins, outs, scratch=()):
    shapes = [jax.ShapeDtypeStruct(shape, dtype) for shape, dtype in outs]
    specs = [SMEM if x.dtype == jnp.int32 else VMEM for x in ins]
    return pl.pallas_call(
        kernel,
        out_shape=shapes,
        in_specs=specs,
        out_specs=[VMEM] * len(shapes),
        scratch_shapes=list(scratch),
        compiler_params=PARAMS,
    )(*ins)


def apply_h(left, right_ref, field, mask):
    def parts(x):
        high = x.astype(bf16)
        return high, (x - high.astype(f32)).astype(bf16)

    high, low = parts(field)
    product = jnp.dot(left, spread_blocks(high, mask), preferred_element_type=f32)
    product = product + jnp.dot(left, spread_blocks(low, mask), preferred_element_type=f32)
    high, low = parts(product)
    total = jnp.zeros((2 * B, LANES), f32)
    for w in range(W_BOND):
        rows = slice(w * B, (w + 1) * B)
        both = jnp.concatenate([high[rows], low[rows]], axis=0)
        total = total + jnp.dot(
            both, spread_blocks(right_ref[rows, :], mask), preferred_element_type=f32
        )
    return total[:B] + total[B:]


def dot_all(former, latter):
    return jnp.sum(former * latter, axis=(0, 1), keepdims=True)


def send_sums(sums, sent_ref):
    lane = iota((1, 128), 1)
    row = jnp.zeros((1, 128), f32)
    for k, entry in enumerate(sums):
        row = jnp.where(lane == k, entry, row)
    sent_ref[...] = jnp.broadcast_to(row[None], (N_SECTOR, 1, 128))


def take_sums(got_ref, count):
    total = jnp.sum(got_ref[...], axis=0)
    return [total[:, k : k + 1] / COUNT_ALL for k in range(count)]


def live(extent_ref):
    extent = extent_ref[0:1, :].astype(jnp.int32)
    row, lane = iota((B, LANES), 0), iota((B, LANES), 1) % B
    return jnp.where((row < extent) & (lane < extent), 1.0, 0.0)


def start_kernel(last_ref, packed_ref, first_ref, right_ref, psi_ref, extent_ref, *rest):
    left_ref, start_ref, image_ref, precond_ref, sent_ref, wide_ref = rest

    @pl.when(last_ref[0] > 0)
    def _():
        write_tall(last_ref[1], packed_ref.at[0], packed_ref.at[1], wide_ref, left_ref)

    @pl.when(last_ref[0] == 0)
    def _():
        left_ref[...] = first_ref[...]

    mask = block_mask(LANES, LANES)
    left = left_ref[...]
    alive = live(extent_ref)
    start = psi_ref[...].astype(f32) * alive
    image = apply_h(left, right_ref, start, mask) * alive
    diagonal = jnp.where(iota((B, LANES), 0) == iota((B, LANES), 1) % B, 1.0, 0.0)
    picked = jnp.concatenate([diagonal.astype(bf16)] * W_BOND, axis=0) * left
    left_diag = jnp.dot(picked, mask, preferred_element_type=f32)
    precond = jnp.zeros((B, LANES), f32)
    for w in range(W_BOND):
        rows = slice(w * B, (w + 1) * B)
        right_diag = jnp.sum(right_ref[rows, :].astype(f32) * diagonal, axis=0, keepdims=True)
        precond = precond + left_diag[rows] * right_diag
    start_ref[...] = start
    image_ref[...] = image
    precond_ref[...] = precond
    send_sums([dot_all(start, start), dot_all(start, image)], sent_ref)


def next_correction(vector, image, energy, precond, left_ref, right_ref, alive, outs):
    vector_ref, image_ref, correction_ref, lifted_ref, sent_ref = outs
    residue = image - energy * vector
    correction = residue / jnp.maximum(precond - energy, 1.0)
    lifted = apply_h(left_ref[...], right_ref, correction, block_mask(LANES, LANES)) * alive
    vector_ref[...] = vector
    image_ref[...] = image
    correction_ref[...] = correction
    lifted_ref[...] = lifted
    send_sums(
        [
            dot_all(vector, correction),
            dot_all(correction, correction),
            dot_all(vector, vector),
            dot_all(correction, image),
            dot_all(correction, lifted),
            dot_all(vector, lifted),
            dot_all(vector, image),
        ],
        sent_ref,
    )


def one_kernel(got_ref, start_ref, raw_ref, precond_ref, left_ref, right_ref, extent_ref, *outs):
    norm, raw = take_sums(got_ref, 2)
    scale = 1.0 / jnp.sqrt(norm + epsilon)
    next_correction(
        start_ref[...] * scale,
        raw_ref[...] * scale,
        raw * scale * scale,
        precond_ref[...],
        left_ref,
        right_ref,
        live(extent_ref),
        outs,
    )


def rotated(got_ref, vector, image, correction, lifted):
    vc, cc, vv, ci, cl, vl, energy = take_sums(got_ref, 7)
    length_sq = jnp.maximum(cc - 2.0 * vc * vc + vc * vc * vv, 0.0)
    inverse = 1.0 / jnp.sqrt(length_sq + epsilon)
    direction = (correction - vc * vector) * inverse
    applied = (lifted - vc * image) * inverse
    coupling = (ci - vc * energy) * inverse
    crossed = (vl - vc * energy) * inverse
    curvature = (cl - vc * vl - vc * ci + vc * vc * energy) * inverse * inverse
    y, x = -2.0 * coupling, curvature - energy
    size = jnp.maximum(jnp.abs(x), jnp.abs(y))
    flat_case = size == 0.0
    size = jnp.where(flat_case, 1.0, size)
    y, x = y / size, jnp.where(flat_case, 1.0, x / size)
    radius = jnp.sqrt(x * x + y * y)
    large = jnp.sqrt((radius + jnp.abs(x)) / (2.0 * radius))
    small = jnp.abs(y) / (2.0 * radius * large)
    sign = jnp.where(y > 0.0, 1.0, -1.0)
    cosine = jnp.where(x >= 0.0, large, small)
    sine = sign * jnp.where(x >= 0.0, small, large)
    turned_energy = (
        cosine * cosine * energy + cosine * sine * (crossed + coupling) + sine * sine * curvature
    )
    return cosine * vector + sine * direction, cosine * image + sine * applied, turned_energy


def two_kernel(
    got_ref, v_ref, i_ref, c_ref, l_ref, precond_ref, left_ref, right_ref, extent_ref, *outs
):
    vector, image, energy = rotated(got_ref, v_ref[...], i_ref[...], c_ref[...], l_ref[...])
    next_correction(
        vector, image, energy, precond_ref[...], left_ref, right_ref, live(extent_ref), outs
    )


def last_kernel(got_ref, v_ref, i_ref, c_ref, l_ref, ground_ref):
    vector, image, energy = rotated(got_ref, v_ref[...], i_ref[...], c_ref[...], l_ref[...])
    ground_ref[0:B, :] = vector
    ground_ref[B : B + 8, :] = jnp.broadcast_to(energy, (8, LANES))


def slot_ranks(owner_grid):
    places = jnp.arange(owner_grid.shape[1])
    earlier = places[None, :] < places[:, None]
    same_owner = owner_grid[:, :, None] == owner_grid[:, None, :]
    return jnp.sum(jnp.where(same_owner & earlier[None], 1, 0), axis=2).astype(jnp.int32)


def tables(route_owner, route_sector, member):
    owner = route_owner.reshape(N_SECTOR, ROWS)
    worker = route_sector.reshape(N_SECTOR, ROWS)
    rank = slot_ranks(owner)
    slot = lax.dynamic_index_in_dim(owner * CAP + rank, member, 0, keepdims=False)
    mine = (owner == member)[:, None, :] & (rank[:, None, :] == jnp.arange(CAP)[None, :, None])
    target = jnp.sum(jnp.where(mine, worker[:, None, :] + 1, 0), axis=2)
    row = jnp.concatenate([slot, target.reshape(SLOTS)])
    return jnp.pad(row, (0, LANES - row.shape[0])).astype(bf16)


def local(
    env_in, mpo_terms, site_tensors, route_owner, route_sector, live_block_extent, psi, right_env
):
    site, sector = lax.axis_index("site"), lax.axis_index("sector")
    core, group = site % 2, sector // 8
    chain_site = group * 2 + core

    def tall(x):
        return x.reshape(SEC, W_BOND, B, B).transpose(1, 2, 0, 3).reshape(W_BOND * B, LANES)

    blocks = site_tensors.reshape(SEC, PHYS, B, B)
    table = tables(route_owner, route_sector, sector)
    tensors = jnp.concatenate(
        [
            blocks.transpose(1, 2, 0, 3).reshape(PHYS * B, LANES),
            jnp.broadcast_to(table[None], (8, LANES)),
        ],
        axis=0,
    )
    first_env = tall(env_in)
    height = tensors.shape[0]
    arrived = turn(jnp.concatenate([tensors, first_env], axis=0), 0)
    near = jnp.stack([arrived[:height]] + [turn(tensors, step) for step in range(1, 4)])
    chain_env = arrived[height:]
    far = other_core(near)
    sites = jnp.arange(N_SITE)
    places = jnp.where(sites % 2 == core, 0, 4) + (group - sites // 2) % 4
    places = jnp.pad(jnp.concatenate([places, core[None]]), (0, LANES - N_SITE - 1))
    info = jnp.concatenate([near[:, PHYS * B], far[:, PHYS * B]]).astype(jnp.int32)
    info = jnp.concatenate([info, places[None].astype(jnp.int32)])

    own_bonds = lax.dynamic_slice_in_dim(mpo_terms, core * HALF, HALF, axis=2)
    mpo = jnp.repeat(own_bonds.transpose(0, 2, 1).reshape(PHYS * HALF, W_BOND), B, axis=1)

    davidson = jnp.concatenate(
        [
            tall(right_env),
            psi.reshape(SEC, B, B).transpose(1, 0, 2).reshape(B, LANES),
            jnp.broadcast_to(jnp.repeat(live_block_extent, B)[None], (8, LANES)).astype(bf16),
        ],
        axis=0,
    )

    outbox_shape = ((SLOTS, PACK, 128), bf16)
    tall_shape = ((W_BOND * B, LANES), bf16)
    wide_scratch = pltpu.VMEM((LANES, 384), f32)
    for i in range(N_SITE - 1):
        if i == 0:
            (outbox,) = call(first_kernel, [info, mpo, near, far, chain_env], [outbox_shape])
        else:
            (outbox,) = call(
                functools.partial(expand_kernel, i),
                [info, mpo, near, far, mine, other],
                [outbox_shape],
                [pltpu.VMEM(*tall_shape), wide_scratch],
            )
        (mine,) = call(
            functools.partial(collect_kernel, i),
            [info, exchange(outbox)],
            [((SEC, PACK, 128), bf16)],
            [pltpu.VMEM((SEC, PACK, 128), f32)],
        )
        other = other_core(mine)
        halves = jnp.stack([mine, other])
        saved = halves if i == 0 else jnp.where(chain_site == i + 1, halves, saved)
        if i == 0:
            mine, other, davidson = lax.optimization_barrier((mine, other, davidson))
            davidson = turn(davidson, 0)
        if i == 1:
            mine, other, davidson = lax.optimization_barrier((mine, other, davidson))

    right = davidson[: W_BOND * B]
    field, extent = davidson[W_BOND * B : W_BOND * B + B], davidson[W_BOND * B + B :]
    field_shape = ((B, LANES), f32)
    sums_shape = ((N_SECTOR, 1, 128), f32)
    last = jnp.stack([chain_site, core])
    left, start, raw, precond, sent = call(
        start_kernel,
        [last, saved, chain_env, right, field, extent],
        [tall_shape, field_shape, field_shape, field_shape, sums_shape],
        [wide_scratch],
    )
    state = [start, raw]
    for step in range(DAV_ITERS):
        kernel = one_kernel if step == 0 else two_kernel
        *state, sent = call(
            kernel,
            [exchange(sent), *state, precond, left, right, extent],
            [field_shape] * 4 + [sums_shape],
        )
    (result,) = call(last_kernel, [exchange(sent), *state], [((B + 8, LANES), f32)])
    result = turn(result, 0)
    ground = result[:B].reshape(B, SEC, B).transpose(1, 0, 2).reshape(1, SEC, B * B)
    return (ground, result[B, :1])


def solution(mesh):
    in_specs = (
        P("sector", None, None),
        P(),
        P("site", "sector", None, None),
        P("site", None, None, None),
        P("site", None, None),
        P("sector"),
        P("site", "sector", None),
        P("site", "sector", None, None),
    )
    out_specs = (P("site", "sector", None), P("site"))
    return jax.shard_map(local, mesh=mesh, in_specs=in_specs, out_specs=out_specs, check_vma=False)
```

```python
import functools

import jax
import jax.numpy as jnp
from jax import lax
from jax.experimental import pallas as pl
from jax.experimental.pallas import tpu as pltpu
from jax.sharding import PartitionSpec as P

B = 32
W_BOND = 20
HALF = W_BOND // 2
PHYS = 4
SEC = 8
DAV_ITERS = 2
CAP = 2
N_SITE = 8
N_SECTOR = 32
SLOTS = N_SECTOR * CAP
ROWS = SEC * PHYS
LANES = SEC * B
PACK = 56
COUNT_ALL = float(N_SECTOR * SEC * B * B)
epsilon = 1e-06
bf16, f32 = jnp.bfloat16, jnp.float32
BOTH = ("site", "sector")


def flat(high, low_core, group, rest):
    return (high * 2 + low_core) * N_SECTOR + group * 8 + rest


def every_device():
    return [(y, c, g, r) for y in range(4) for c in range(2) for g in range(4) for r in range(8)]


def turn(block, step):
    pairs = [(flat(y, c, g, r), flat(g, c, (y + step) % 4, r)) for y, c, g, r in every_device()]
    return lax.ppermute(block, BOTH, pairs)


def exchange(block):
    groups = [
        [flat(y, c, g, r) for y in range(4) for r in range(8)] for g in range(4) for c in range(2)
    ]
    return lax.all_to_all(block, BOTH, split_axis=0, concat_axis=0, tiled=True, axis_index_groups=groups)


def other_core(block):
    return lax.ppermute(block, "site", [(i, i ^ 1) for i in range(N_SITE)])


def iota(shape, axis):
    return lax.broadcasted_iota(jnp.int32, shape, axis)


def block_mask(rows, lanes):
    same = (iota((rows, lanes), 0) // B) == (iota((rows, lanes), 1) // B)
    return jnp.where(same, 1.0, 0.0).astype(bf16)


def spread_blocks(field, mask):
    return jnp.concatenate([field] * SEC, axis=0) * mask


def column_block():
    return (iota((8, 128), 1) % B) // 8


def half_to_tiles(square):
    cb = column_block()

    def chosen(step, tile):
        parts = [tile[8 * d : 8 * d + 8, :] for d in range(4)]
        picked = parts[(3 + step) % 4]
        for d in (2, 1, 0):
            picked = jnp.where(cb == d, parts[(d + step) % 4], picked)
        return picked

    lane = iota((8, 128), 1)
    s = [[chosen(step, tile) for tile in square] for step in range(3)]
    return [
        s[0][0],
        s[0][1],
        s[1][0],
        s[1][1],
        jnp.where(lane < 64, s[0][2], pltpu.roll(s[1][2], 64, 1)),
        jnp.where(cb < 2, s[2][0], pltpu.roll(s[2][1], 16, 1)),
        s[2][2],
    ]


def tiles_to_half(tiles):
    cb = column_block()
    diag = [tiles[0], tiles[1], tiles[4]]
    near = [tiles[2], tiles[3], pltpu.roll(tiles[4], 64, 1)]
    far = [tiles[5], pltpu.roll(tiles[5], 112, 1), tiles[6]]
    square = []
    for tile in range(3):
        rows = []
        for d in range(4):
            rows.append(
                jnp.where(
                    cb == d, diag[tile], jnp.where(cb == (d - 1) % 4, near[tile], far[tile])
                )
            )
        square.append(jnp.concatenate(rows, axis=0))
    return square


def moved(sources, shifts):
    quarter = iota((B, 128), 1) // B
    total = None
    for k, (source, shift) in enumerate(zip(sources, shifts)):
        shift = shift % 128
        piece = pltpu.roll(source, shift, 1) if shift else source
        total = piece if total is None else jnp.where(quarter == k, piece, total)
    return total


def write_tall(core, mine_ref, other_ref, wide_ref, tall_ref):
    first = jnp.full((PACK, 128), core, jnp.int32) == 0
    ab = iota((B, LANES), 0) // 8
    bb = (iota((B, LANES), 1) % B) // 8
    gap = (ab - bb) & 3
    valid = (gap < 2) | ((gap == 2) & (bb < 2))
    for half in range(2):
        squares = []
        for t in range(SEC):
            mine, other = mine_ref[t].astype(f32), other_ref[t].astype(f32)
            whole = jnp.where(first, mine, other) if half == 0 else jnp.where(first, other, mine)
            square = tiles_to_half([whole[8 * i : 8 * i + 8, :] for i in range(7)])
            squares.append(square)
            for tile in range(3):
                wide_ref[t * B : (t + 1) * B, tile * 128 : (tile + 1) * 128] = square[tile]
        turned = jnp.transpose(wide_ref[...])
        bonds = []
        for v in range(HALF):
            tile, offset = v // 4, (v % 4) * B
            straight = jnp.concatenate(
                [
                    moved(
                        [squares[4 * q + k][tile] for k in range(4)],
                        [k * B - offset for k in range(4)],
                    )
                    for q in range(2)
                ],
                axis=1,
            )
            bonds.append(jnp.where(valid, straight, turned[v * B : (v + 1) * B, :]))
        for d in range(4):
            for v in range(0, HALF, 2):
                pair = [bonds[v + k][8 * d : 8 * d + 8, :] for k in range(2)]
                start = (d * W_BOND + half * HALF + v) * 8
                tall_ref[start : start + 16, :] = jnp.concatenate(pair, axis=0).astype(bf16)


def bond_rows(tall, bond, bonds=W_BOND):
    return jnp.concatenate(
        [tall[(d * bonds + bond) * 8 : (d * bonds + bond) * 8 + 8, :] for d in range(4)], axis=0
    )


def join_cores(core, near_ref, far_ref, tall_ref):
    first = jnp.full((HALF * B, LANES), core, jnp.int32) == 0
    near, far = near_ref[...].astype(f32), far_ref[...].astype(f32)
    low, high = jnp.where(first, near, far).astype(bf16), jnp.where(first, far, near).astype(bf16)
    step = HALF * 8
    for d in range(4):
        tall_ref[2 * d * step : (2 * d + 1) * step, :] = low[d * step : (d + 1) * step]
        tall_ref[(2 * d + 1) * step : (2 * d + 2) * step, :] = high[d * step : (d + 1) * step]


def contract_rows(i, info_ref, mpo_ref, tensor_ref, far_tensor_ref, tall, out_ref):
    place = info_ref[N_SITE, i]
    near_core = jnp.full((B, LANES), place, jnp.int32) < 4
    turned = place & 3
    mask = block_mask(LANES, LANES)
    mixer = mpo_ref[...]
    step = W_BOND * 8
    mixes = [
        jnp.dot(mixer, tall[d * step : (d + 1) * step, :], preferred_element_type=f32).astype(bf16)
        for d in range(4)
    ]
    for p in range(PHYS):
        mixed = jnp.concatenate(
            [mix[p * HALF * 8 : (p + 1) * HALF * 8, :] for mix in mixes], axis=0
        )
        rows = slice(p * B, (p + 1) * B)
        tensor = jnp.where(
            near_core, tensor_ref[turned, rows, :].astype(f32), far_tensor_ref[turned, rows, :].astype(f32)
        )
        right = spread_blocks(tensor.astype(bf16), mask)
        halfway = jnp.dot(mixed, right, preferred_element_type=f32)
        bonds = [bond_rows(halfway, v, HALF).astype(bf16) for v in range(HALF)]
        wide = []
        for s in range(SEC):
            source, offset = (s // 4) * 128, (s % 4) * B
            tiles = []
            for tile in range(3):
                here = [v for v in range(4 * tile, 4 * tile + 4) if v < HALF]
                tiles.append(
                    moved(
                        [bonds[v][:, source : source + 128] for v in here],
                        [(v % 4) * B - offset for v in here],
                    )
                )
            wide.append(jnp.concatenate(tiles, axis=1))
        wide = jnp.concatenate(wide, axis=0)
        blocks = lax.dot_general(right, wide, (((0,), (0,)), ((), ())), preferred_element_type=f32)
        for s in range(SEC):
            tiles = half_to_tiles(
                [blocks[s * B : (s + 1) * B, tile * 128 : (tile + 1) * 128] for tile in range(3)]
            )
            out_ref[info_ref[place, s * PHYS + p]] = jnp.concatenate(tiles, axis=0).astype(bf16)


def first_kernel(info_ref, mpo_ref, tensor_ref, far_tensor_ref, near_ref, far_ref, *rest):
    out_ref, tall_ref = rest
    join_cores(info_ref[N_SITE, N_SITE], near_ref, far_ref, tall_ref)
    contract_rows(0, info_ref, mpo_ref, tensor_ref, far_tensor_ref, tall_ref[...], out_ref)


def expand_kernel(i, info_ref, mpo_ref, tensor_ref, far_tensor_ref, mine_ref, other_ref, *rest):
    out_ref, tall_ref, wide_ref = rest
    write_tall(info_ref[N_SITE, N_SITE], mine_ref, other_ref, wide_ref, tall_ref)
    contract_rows(i, info_ref, mpo_ref, tensor_ref, far_tensor_ref, tall_ref[...], out_ref)


def collect_kernel(i, info_ref, inbox_ref, out_ref, total_ref):
    place = info_ref[N_SITE, i]
    total_ref[...] = jnp.zeros_like(total_ref)
    def take(turn_index, carry):
        for k in range(4):
            q = turn_index * 4 + k
            t = info_ref[place, ROWS + q]

            @pl.when(t > 0)
            def _():
                total_ref[t - 1] += inbox_ref[q].astype(f32)

        return carry

    lax.fori_loop(0, SLOTS // 4, take, 0)
    out_ref[...] = total_ref[...].astype(bf16)


VMEM = pl.BlockSpec(memory_space=pltpu.VMEM)
SMEM = pl.BlockSpec(memory_space=pltpu.SMEM)
PARAMS = pltpu.CompilerParams(vmem_limit_bytes=48 << 20)


def call(kernel, ins, outs, scratch=()):
    shapes = [jax.ShapeDtypeStruct(shape, dtype) for shape, dtype in outs]
    specs = [SMEM if x.dtype == jnp.int32 else VMEM for x in ins]
    return pl.pallas_call(
        kernel,
        out_shape=shapes,
        in_specs=specs,
        out_specs=[VMEM] * len(shapes),
        scratch_shapes=list(scratch),
        compiler_params=PARAMS,
        name=getattr(kernel, "func", kernel).__name__,
    )(*ins)


def run_expand(i, info, mpo, near, far, mine, other):
    (outbox,) = call(
        functools.partial(expand_kernel, i),
        [info, mpo, near, far, mine, other],
        [((SLOTS, PACK, 128), bf16)],
        [pltpu.VMEM((W_BOND * B, LANES), bf16), pltpu.VMEM((LANES, 384), f32)],
    )
    return outbox


def run_collect(i, info, inbox):
    (mine,) = call(
        functools.partial(collect_kernel, i),
        [info, inbox],
        [((SEC, PACK, 128), bf16)],
        [pltpu.VMEM((SEC, PACK, 128), f32)],
    )
    return mine


def apply_h(left, right_ref, field, mask):
    def parts(x):
        high = x.astype(bf16)
        return high, (x - high.astype(f32)).astype(bf16)

    high, low = parts(field)
    product = jnp.dot(left, spread_blocks(high, mask), preferred_element_type=f32)
    product = product + jnp.dot(left, spread_blocks(low, mask), preferred_element_type=f32)
    total = jnp.zeros((2 * B, LANES), f32)
    for w in range(W_BOND):
        rows = slice(w * B, (w + 1) * B)
        both = jnp.concatenate(parts(bond_rows(product, w)), axis=0)
        total = total + jnp.dot(
            both, spread_blocks(right_ref[rows, :], mask), preferred_element_type=f32
        )
    return total[:B] + total[B:]


def dot_all(former, latter):
    return jnp.sum(former * latter, axis=(0, 1), keepdims=True)


def send_sums(sums, sent_ref):
    lane = iota((1, 128), 1)
    row = jnp.zeros((1, 128), f32)
    for k, entry in enumerate(sums):
        row = jnp.where(lane == k, entry, row)
    sent_ref[...] = jnp.broadcast_to(row[None], (N_SECTOR, 1, 128))


def take_sums(got_ref, count):
    total = jnp.sum(got_ref[...], axis=0)
    return [total[:, k : k + 1] / COUNT_ALL for k in range(count)]


def live(extent_ref):
    extent = extent_ref[0:1, :].astype(jnp.int32)
    row, lane = iota((B, LANES), 0), iota((B, LANES), 1) % B
    return jnp.where((row < extent) & (lane < extent), 1.0, 0.0)


def start_kernel(last_ref, packed_ref, near_ref, far_ref, right_ref, psi_ref, extent_ref, *rest):
    left_ref, start_ref, image_ref, precond_ref, sent_ref, wide_ref = rest

    @pl.when(last_ref[0] > 0)
    def _():
        write_tall(last_ref[1], packed_ref.at[0], packed_ref.at[1], wide_ref, left_ref)

    @pl.when(last_ref[0] == 0)
    def _():
        join_cores(last_ref[1], near_ref, far_ref, left_ref)

    mask = block_mask(LANES, LANES)
    left = left_ref[...]
    alive = live(extent_ref)
    start = psi_ref[...].astype(f32) * alive
    image = apply_h(left, right_ref, start, mask) * alive
    diagonal = jnp.where(iota((B, LANES), 0) == iota((B, LANES), 1) % B, 1.0, 0.0)
    tall_row = iota((W_BOND * B, LANES), 0)
    tall_row = (tall_row // (W_BOND * 8)) * 8 + tall_row % 8
    on_diagonal = jnp.where(tall_row == iota((W_BOND * B, LANES), 1) % B, 1.0, 0.0)
    picked = on_diagonal.astype(bf16) * left
    left_diag = jnp.dot(picked, mask, preferred_element_type=f32)
    precond = jnp.zeros((B, LANES), f32)
    for w in range(W_BOND):
        rows = slice(w * B, (w + 1) * B)
        right_diag = jnp.sum(right_ref[rows, :].astype(f32) * diagonal, axis=0, keepdims=True)
        precond = precond + bond_rows(left_diag, w) * right_diag
    start_ref[...] = start
    image_ref[...] = image
    precond_ref[...] = precond
    send_sums([dot_all(start, start), dot_all(start, image)], sent_ref)


def next_correction(vector, image, energy, precond, left_ref, right_ref, alive, outs):
    vector_ref, image_ref, correction_ref, lifted_ref, sent_ref = outs
    residue = image - energy * vector
    correction = residue / jnp.maximum(precond - energy, 1.0)
    lifted = apply_h(left_ref[...], right_ref, correction, block_mask(LANES, LANES)) * alive
    vector_ref[...] = vector
    image_ref[...] = image
    correction_ref[...] = correction
    lifted_ref[...] = lifted
    send_sums(
        [
            dot_all(vector, correction),
            dot_all(correction, correction),
            dot_all(vector, vector),
            dot_all(correction, image),
            dot_all(correction, lifted),
            dot_all(vector, lifted),
            dot_all(vector, image),
        ],
        sent_ref,
    )


def one_kernel(got_ref, start_ref, raw_ref, precond_ref, left_ref, right_ref, extent_ref, *outs):
    norm, raw = take_sums(got_ref, 2)
    scale = 1.0 / jnp.sqrt(norm + epsilon)
    next_correction(
        start_ref[...] * scale,
        raw_ref[...] * scale,
        raw * scale * scale,
        precond_ref[...],
        left_ref,
        right_ref,
        live(extent_ref),
        outs,
    )


def rotated(got_ref, vector, image, correction, lifted):
    vc, cc, vv, ci, cl, vl, energy = take_sums(got_ref, 7)
    length_sq = jnp.maximum(cc - 2.0 * vc * vc + vc * vc * vv, 0.0)
    inverse = 1.0 / jnp.sqrt(length_sq + epsilon)
    direction = (correction - vc * vector) * inverse
    applied = (lifted - vc * image) * inverse
    coupling = (ci - vc * energy) * inverse
    crossed = (vl - vc * energy) * inverse
    curvature = (cl - vc * vl - vc * ci + vc * vc * energy) * inverse * inverse
    y, x = -2.0 * coupling, curvature - energy
    size = jnp.maximum(jnp.abs(x), jnp.abs(y))
    flat_case = size == 0.0
    size = jnp.where(flat_case, 1.0, size)
    y, x = y / size, jnp.where(flat_case, 1.0, x / size)
    radius = jnp.sqrt(x * x + y * y)
    large = jnp.sqrt((radius + jnp.abs(x)) / (2.0 * radius))
    small = jnp.abs(y) / (2.0 * radius * large)
    sign = jnp.where(y > 0.0, 1.0, -1.0)
    cosine = jnp.where(x >= 0.0, large, small)
    sine = sign * jnp.where(x >= 0.0, small, large)
    turned_energy = (
        cosine * cosine * energy + cosine * sine * (crossed + coupling) + sine * sine * curvature
    )
    return cosine * vector + sine * direction, cosine * image + sine * applied, turned_energy


def two_kernel(
    got_ref, v_ref, i_ref, c_ref, l_ref, precond_ref, left_ref, right_ref, extent_ref, *outs
):
    vector, image, energy = rotated(got_ref, v_ref[...], i_ref[...], c_ref[...], l_ref[...])
    next_correction(
        vector, image, energy, precond_ref[...], left_ref, right_ref, live(extent_ref), outs
    )


def last_kernel(got_ref, v_ref, i_ref, c_ref, l_ref, ground_ref):
    vector, image, energy = rotated(got_ref, v_ref[...], i_ref[...], c_ref[...], l_ref[...])
    ground_ref[0:B, :] = vector
    ground_ref[B : B + 8, :] = jnp.broadcast_to(energy, (8, LANES))


def slot_ranks(owner_grid):
    places = jnp.arange(owner_grid.shape[1])
    earlier = places[None, :] < places[:, None]
    same_owner = owner_grid[:, :, None] == owner_grid[:, None, :]
    return jnp.sum(jnp.where(same_owner & earlier[None], 1, 0), axis=2).astype(jnp.int32)


def tables(route_owner, route_sector, member):
    owner = route_owner.reshape(N_SECTOR, ROWS)
    worker = route_sector.reshape(N_SECTOR, ROWS)
    rank = slot_ranks(owner)
    slot = lax.dynamic_index_in_dim(owner * CAP + rank, member, 0, keepdims=False)
    mine = (owner == member)[:, None, :] & (rank[:, None, :] == jnp.arange(CAP)[None, :, None])
    target = jnp.sum(jnp.where(mine, worker[:, None, :] + 1, 0), axis=2)
    row = jnp.concatenate([slot, target.reshape(SLOTS)])
    return jnp.pad(row, (0, LANES - row.shape[0])).astype(bf16)


def local(
    env_in, mpo_terms, site_tensors, route_owner, route_sector, live_block_extent, psi, right_env
):
    site, sector = lax.axis_index("site"), lax.axis_index("sector")
    core, group = site % 2, sector // 8
    chain_site = group * 2 + core

    def tall(x):
        return x.reshape(SEC, W_BOND, B, B).transpose(1, 2, 0, 3).reshape(W_BOND * B, LANES)

    blocks = site_tensors.reshape(SEC, PHYS, B, B)
    table = tables(route_owner, route_sector, sector)
    tensors = jnp.concatenate(
        [
            blocks.transpose(1, 2, 0, 3).reshape(PHYS * B, LANES),
            jnp.broadcast_to(table[None], (8, LANES)),
        ],
        axis=0,
    )
    own_env = lax.dynamic_slice_in_dim(env_in, core * HALF, HALF, axis=1)
    own_env = own_env.reshape(SEC, HALF, 4, 8, B).transpose(2, 1, 3, 0, 4).reshape(HALF * B, LANES)
    near = jnp.stack([turn(tensors, step) for step in range(4)])
    near_env = turn(own_env, 0)
    far, far_env = other_core(near), other_core(near_env)
    sites = jnp.arange(N_SITE)
    places = jnp.where(sites % 2 == core, 0, 4) + (group - sites // 2) % 4
    places = jnp.pad(jnp.concatenate([places, core[None]]), (0, LANES - N_SITE - 1))
    info = jnp.concatenate([near[:, PHYS * B], far[:, PHYS * B]]).astype(jnp.int32)
    info = jnp.concatenate([info, places[None].astype(jnp.int32)])

    own_bonds = lax.dynamic_slice_in_dim(mpo_terms, core * HALF, HALF, axis=2)
    mpo = own_bonds.transpose(0, 2, 1).reshape(PHYS * HALF, 1, W_BOND, 1) * jnp.eye(8, dtype=bf16)[None, :, None, :]
    mpo = mpo.reshape(PHYS * HALF * 8, W_BOND * 8)

    davidson = jnp.concatenate(
        [
            tall(right_env),
            psi.reshape(SEC, B, B).transpose(1, 0, 2).reshape(B, LANES),
            jnp.broadcast_to(jnp.repeat(live_block_extent, B)[None], (8, LANES)).astype(bf16),
        ],
        axis=0,
    )

    outbox_shape = ((SLOTS, PACK, 128), bf16)
    tall_shape = ((W_BOND * B, LANES), bf16)
    wide_scratch = pltpu.VMEM((LANES, 384), f32)
    for i in range(N_SITE - 1):
        if i == 0:
            (outbox,) = call(first_kernel, [info, mpo, near, far, near_env, far_env], [outbox_shape], [pltpu.VMEM(*tall_shape)])
        else:
            outbox = run_expand(i, info, mpo, near, far, mine, other)
        mine = run_collect(i, info, exchange(outbox))
        other = other_core(mine)
        halves = jnp.stack([mine, other])
        saved = halves if i == 0 else jnp.where(chain_site == i + 1, halves, saved)
        if i == 0:
            mine, other, davidson = lax.optimization_barrier((mine, other, davidson))
            davidson = turn(davidson, 0)
        if i == 1:
            mine, other, davidson = lax.optimization_barrier((mine, other, davidson))

    right = davidson[: W_BOND * B]
    field, extent = davidson[W_BOND * B : W_BOND * B + B], davidson[W_BOND * B + B :]
    field_shape = ((B, LANES), f32)
    sums_shape = ((N_SECTOR, 1, 128), f32)
    last = jnp.stack([chain_site, core])
    left, start, raw, precond, sent = call(
        start_kernel,
        [last, saved, near_env, far_env, right, field, extent],
        [tall_shape, field_shape, field_shape, field_shape, sums_shape],
        [wide_scratch],
    )
    state = [start, raw]
    for step in range(DAV_ITERS):
        kernel = one_kernel if step == 0 else two_kernel
        *state, sent = call(
            kernel,
            [exchange(sent), *state, precond, left, right, extent],
            [field_shape] * 4 + [sums_shape],
        )
    (result,) = call(last_kernel, [exchange(sent), *state], [((B + 8, LANES), f32)])
    result = turn(result, 0)
    ground = result[:B].reshape(B, SEC, B).transpose(1, 0, 2).reshape(1, SEC, B * B)
    return (ground, result[B, :1])


def solution(mesh):
    in_specs = (
        P("sector", None, None),
        P(),
        P("site", "sector", None, None),
        P("site", None, None, None),
        P("site", None, None),
        P("sector"),
        P("site", "sector", None),
        P("site", "sector", None, None),
    )
    out_specs = (P("site", "sector", None), P("site"))
    return jax.shard_map(local, mesh=mesh, in_specs=in_specs, out_specs=out_specs, check_vma=False)
```

```python
import functools

import jax
import jax.numpy as jnp
from jax import lax
from jax.experimental import pallas as pl
from jax.experimental.pallas import tpu as pltpu
from jax.sharding import PartitionSpec as P

B = 32
W_BOND = 20
HALF = W_BOND // 2
PHYS = 4
SEC = 8
DAV_ITERS = 2
CAP = 2
N_SITE = 8
N_SECTOR = 32
SLOTS = N_SECTOR * CAP
ROWS = SEC * PHYS
LANES = SEC * B
PACK = 48
COUNT_ALL = float(N_SECTOR * SEC * B * B)
epsilon = 1e-06
bf16, f32 = jnp.bfloat16, jnp.float32
BOTH = ("site", "sector")


def flat(high, low_core, group, rest):
    return (high * 2 + low_core) * N_SECTOR + group * 8 + rest


def every_device():
    return [(y, c, g, r) for y in range(4) for c in range(2) for g in range(4) for r in range(8)]


def turn(block, step):
    pairs = [(flat(y, c, g, r), flat(g, c, (y + step) % 4, r)) for y, c, g, r in every_device()]
    return lax.ppermute(block, BOTH, pairs)


def exchange(block):
    groups = [
        [flat(y, c, g, r) for y in range(4) for r in range(8)] for g in range(4) for c in range(2)
    ]
    return lax.all_to_all(block, BOTH, split_axis=0, concat_axis=0, tiled=True, axis_index_groups=groups)


def other_core(block):
    return lax.ppermute(block, "site", [(i, i ^ 1) for i in range(N_SITE)])


def iota(shape, axis):
    return lax.broadcasted_iota(jnp.int32, shape, axis)


def block_mask(rows, lanes):
    same = (iota((rows, lanes), 0) // B) == (iota((rows, lanes), 1) // B)
    return jnp.where(same, 1.0, 0.0).astype(bf16)


def spread_blocks(field, mask):
    return jnp.concatenate([field] * SEC, axis=0) * mask


def column_block():
    return (iota((8, 128), 1) % B) // 8


def lane_map(sources):
    return jnp.where(iota((128, 256), 0) == sources, 1.0, 0.0).astype(bf16)


def outward():
    lane = iota((128, 256), 1)
    inner = lane % 128
    source = ((inner // B) % 2) * B + 4 * ((inner % B) // 8) + inner % 4
    used = (inner % 8 >= 4) & ((inner < 64) == (lane < 128))
    return lane_map(jnp.where(used, source, -1))


def inward():
    lane = iota((128, 256), 1)
    inner = lane % 128
    source = (inner // B) * B + 8 * ((inner % B) // 4) + 4 + inner % 4
    used = (inner < 64) & (inner % B < 16)
    return lane_map(jnp.where(used, source + jnp.where(lane < 128, 0, 64), -1))


def relocated(tiles, matrix):
    stacked = jnp.concatenate(tiles, axis=0).astype(bf16)
    images = jnp.dot(stacked, matrix, preferred_element_type=f32)
    rows = [slice(8 * k, 8 * k + 8) for k in range(len(tiles))]
    return [(images[r, :128], images[r, 128:]) for r in rows]


def halves_to_tiles(squares, matrix):
    cb, lane = column_block(), iota((8, 128), 1)

    def chosen(step, tile):
        parts = [tile[8 * d : 8 * d + 8, :] for d in range(4)]
        picked = parts[(3 + step) % 4]
        for d in (2, 1, 0):
            picked = jnp.where(cb == d, parts[(d + step) % 4], picked)
        return picked

    extras = relocated([chosen(2, square[2]) for square in squares], matrix)
    for (first, second, third), (low, high) in zip(squares, extras):
        near = pltpu.roll(chosen(1, third), 64, 1)
        yield [
            jnp.where(repeated(), low + pltpu.roll(high, 4, 0), chosen(0, first)),
            chosen(0, second),
            chosen(1, first),
            chosen(1, second),
            jnp.where(lane < 64, chosen(0, third), near),
            jnp.where(cb < 2, chosen(2, first), pltpu.roll(chosen(2, second), 16, 1)),
        ]


def repeated():
    return (iota((8, 128), 0) < 4) & (iota((8, 128), 1) % 8 >= 4)


def tiles_to_half(tiles, extra):
    cb = column_block()
    diag = [tiles[0], tiles[1], tiles[4]]
    near = [tiles[2], tiles[3], pltpu.roll(tiles[4], 64, 1)]
    low, high = extra
    extra = jnp.where(iota((8, 128), 0) < 4, low, pltpu.roll(high, 4, 0))
    far = [tiles[5], pltpu.roll(tiles[5], 112, 1), extra]
    square = []
    for tile in range(3):
        rows = []
        for d in range(4):
            rows.append(
                jnp.where(
                    cb == d, diag[tile], jnp.where(cb == (d - 1) % 4, near[tile], far[tile])
                )
            )
        square.append(jnp.concatenate(rows, axis=0))
    return square


def moved(sources, shifts):
    quarter = iota((B, 128), 1) // B
    total = None
    for k, (source, shift) in enumerate(zip(sources, shifts)):
        shift = shift % 128
        piece = pltpu.roll(source, shift, 1) if shift else source
        total = piece if total is None else jnp.where(quarter == k, piece, total)
    return total


def write_tall(core, mine_ref, other_ref, wide_ref, tall_ref):
    first = jnp.full((PACK, 128), core, jnp.int32) == 0
    ab = iota((B, LANES), 0) // 8
    bb = (iota((B, LANES), 1) % B) // 8
    gap = (ab - bb) & 3
    spare = (gap == 0) & (iota((B, LANES), 0) % 8 < 4) & (iota((B, LANES), 1) % 8 >= 4)
    matrix = inward()
    valid = ((gap < 2) & jnp.logical_not(spare)) | ((gap == 2) & (bb < 2))
    for half in range(2):
        def part(t, rows):
            mine, other = mine_ref[t, rows, :].astype(f32), other_ref[t, rows, :].astype(f32)
            here = first[rows]
            return jnp.where(here, mine, other) if half == 0 else jnp.where(here, other, mine)

        squares = []
        extras = relocated([part(t, slice(0, 16))[:8] for t in range(SEC)], matrix)
        for t in range(SEC):
            whole = part(t, slice(0, PACK))
            square = tiles_to_half([whole[8 * i : 8 * i + 8, :] for i in range(6)], extras[t])
            squares.append(square)
            for tile in range(3):
                wide_ref[t * B : (t + 1) * B, tile * 128 : (tile + 1) * 128] = square[tile]
        turned = jnp.transpose(wide_ref[...])
        bonds = []
        for v in range(HALF):
            tile, offset = v // 4, (v % 4) * B
            straight = jnp.concatenate(
                [
                    moved(
                        [squares[4 * q + k][tile] for k in range(4)],
                        [k * B - offset for k in range(4)],
                    )
                    for q in range(2)
                ],
                axis=1,
            )
            bonds.append(jnp.where(valid, straight, turned[v * B : (v + 1) * B, :]))
        for d in range(4):
            for v in range(0, HALF, 2):
                pair = [bonds[v + k][8 * d : 8 * d + 8, :] for k in range(2)]
                start = (d * W_BOND + half * HALF + v) * 8
                tall_ref[start : start + 16, :] = jnp.concatenate(pair, axis=0).astype(bf16)


def bond_rows(tall, bond, bonds=W_BOND):
    return jnp.concatenate(
        [tall[(d * bonds + bond) * 8 : (d * bonds + bond) * 8 + 8, :] for d in range(4)], axis=0
    )


def join_cores(core, near_ref, far_ref, tall_ref):
    first = jnp.full((HALF * B, LANES), core, jnp.int32) == 0
    near, far = near_ref[...].astype(f32), far_ref[...].astype(f32)
    low, high = jnp.where(first, near, far).astype(bf16), jnp.where(first, far, near).astype(bf16)
    step = HALF * 8
    for d in range(4):
        tall_ref[2 * d * step : (2 * d + 1) * step, :] = low[d * step : (d + 1) * step]
        tall_ref[(2 * d + 1) * step : (2 * d + 2) * step, :] = high[d * step : (d + 1) * step]


def contract_rows(step, info_ref, mpo_ref, tensor_ref, far_tensor_ref, tall, out_ref):
    place = info_ref[N_SITE, step]
    near_core = jnp.full((B, LANES), place, jnp.int32) < 4
    turned = place & 3
    mask = block_mask(LANES, LANES)
    mixer, matrix = mpo_ref[...], outward()
    step = W_BOND * 8
    mixes = [
        jnp.dot(mixer, tall[d * step : (d + 1) * step, :], preferred_element_type=f32).astype(bf16)
        for d in range(4)
    ]
    for p in range(PHYS):
        mixed = jnp.concatenate(
            [mix[p * HALF * 8 : (p + 1) * HALF * 8, :] for mix in mixes], axis=0
        )
        rows = slice(p * B, (p + 1) * B)
        tensor = jnp.where(
            near_core, tensor_ref[turned, rows, :].astype(f32), far_tensor_ref[turned, rows, :].astype(f32)
        )
        right = spread_blocks(tensor.astype(bf16), mask)
        halfway = jnp.dot(mixed, right, preferred_element_type=f32)
        bonds = [bond_rows(halfway, v, HALF).astype(bf16) for v in range(HALF)]
        wide = []
        for s in range(SEC):
            source, offset = (s // 4) * 128, (s % 4) * B
            tiles = []
            for tile in range(3):
                here = [v for v in range(4 * tile, 4 * tile + 4) if v < HALF]
                tiles.append(
                    moved(
                        [bonds[v][:, source : source + 128] for v in here],
                        [(v % 4) * B - offset for v in here],
                    )
                )
            wide.append(jnp.concatenate(tiles, axis=1))
        wide = jnp.concatenate(wide, axis=0)
        blocks = lax.dot_general(right, wide, (((0,), (0,)), ((), ())), preferred_element_type=f32)
        squares = [
            [blocks[s * B : (s + 1) * B, tile * 128 : (tile + 1) * 128] for tile in range(3)]
            for s in range(SEC)
        ]
        for s, tiles in enumerate(halves_to_tiles(squares, matrix)):
            out_ref[info_ref[place, s * PHYS + p]] = jnp.concatenate(tiles, axis=0).astype(bf16)


def first_kernel(info_ref, mpo_ref, tensor_ref, far_tensor_ref, near_ref, far_ref, *rest):
    out_ref, tall_ref = rest
    join_cores(info_ref[N_SITE, N_SITE], near_ref, far_ref, tall_ref)
    contract_rows(0, info_ref, mpo_ref, tensor_ref, far_tensor_ref, tall_ref[...], out_ref)


def expand_kernel(step_ref, info_ref, mpo_ref, tensor_ref, far_tensor_ref, mine_ref, other_ref, *rest):
    out_ref, tall_ref, wide_ref = rest
    write_tall(info_ref[N_SITE, N_SITE], mine_ref, other_ref, wide_ref, tall_ref)
    contract_rows(step_ref[0], info_ref, mpo_ref, tensor_ref, far_tensor_ref, tall_ref[...], out_ref)


def collect_kernel(step_ref, info_ref, inbox_ref, out_ref, total_ref):
    place = info_ref[N_SITE, step_ref[0]]
    total_ref[...] = jnp.zeros_like(total_ref)
    def take(turn_index, carry):
        for k in range(4):
            q = turn_index * 4 + k
            t = info_ref[place, ROWS + q]

            @pl.when(t > 0)
            def _():
                total_ref[t - 1] += inbox_ref[q].astype(f32)

        return carry

    lax.fori_loop(0, SLOTS // 4, take, 0)
    out_ref[...] = total_ref[...].astype(bf16)


VMEM = pl.BlockSpec(memory_space=pltpu.VMEM)
SMEM = pl.BlockSpec(memory_space=pltpu.SMEM)
PARAMS = pltpu.CompilerParams(vmem_limit_bytes=48 << 20)


def call(kernel, ins, outs, scratch=()):
    shapes = [jax.ShapeDtypeStruct(shape, dtype) for shape, dtype in outs]
    specs = [SMEM if x.dtype == jnp.int32 else VMEM for x in ins]
    return pl.pallas_call(
        kernel,
        out_shape=shapes,
        in_specs=specs,
        out_specs=[VMEM] * len(shapes),
        scratch_shapes=list(scratch),
        compiler_params=PARAMS,
        name=getattr(kernel, "func", kernel).__name__,
    )(*ins)


def run_expand(i, info, mpo, near, far, mine, other):
    (outbox,) = call(
        expand_kernel,
        [i, info, mpo, near, far, mine, other],
        [((SLOTS, PACK, 128), bf16)],
        [pltpu.VMEM((W_BOND * B, LANES), bf16), pltpu.VMEM((LANES, 384), f32)],
    )
    return outbox


def run_collect(i, info, inbox):
    (mine,) = call(
        collect_kernel,
        [i, info, inbox],
        [((SEC, PACK, 128), bf16)],
        [pltpu.VMEM((SEC, PACK, 128), f32)],
    )
    return mine


def apply_h(left, right_ref, field, mask, product_ref):
    def parts(x):
        high = x.astype(bf16)
        return high, (x - high.astype(f32)).astype(bf16)

    high, low = parts(field)
    product = jnp.dot(left, spread_blocks(high, mask), preferred_element_type=f32)
    product = product + jnp.dot(left, spread_blocks(low, mask), preferred_element_type=f32)
    product_ref[...] = product

    def one_group(group, total):
        for k in range(5):
            w = group * 5 + k
            piece = jnp.concatenate(
                [product_ref[pl.ds((d * W_BOND + w) * 8, 8), :] for d in range(4)], axis=0
            )
            both = jnp.concatenate(parts(piece), axis=0)
            right = right_ref[pl.ds(pl.multiple_of(w * B, B), B), :]
            total = total + jnp.dot(both, spread_blocks(right, mask), preferred_element_type=f32)
        return total

    total = lax.fori_loop(0, W_BOND // 5, one_group, jnp.zeros((2 * B, LANES), f32))
    return total[:B] + total[B:]


def dot_all(former, latter):
    return jnp.sum(former * latter, axis=(0, 1), keepdims=True)


def send_sums(sums, sent_ref):
    lane = iota((1, 128), 1)
    row = jnp.zeros((1, 128), f32)
    for k, entry in enumerate(sums):
        row = jnp.where(lane == k, entry, row)
    sent_ref[...] = jnp.broadcast_to(row[None], (N_SECTOR, 1, 128))


def take_sums(got_ref, count):
    total = jnp.sum(got_ref[...], axis=0)
    return [total[:, k : k + 1] / COUNT_ALL for k in range(count)]


def live(extent_ref):
    extent = extent_ref[0:1, :].astype(jnp.int32)
    row, lane = iota((B, LANES), 0), iota((B, LANES), 1) % B
    return jnp.where((row < extent) & (lane < extent), 1.0, 0.0)


def start_kernel(last_ref, packed_ref, near_ref, far_ref, right_ref, psi_ref, extent_ref, *rest):
    left_ref, start_ref, image_ref, precond_ref, sent_ref, wide_ref, product_ref = rest

    @pl.when(last_ref[0] > 0)
    def _():
        write_tall(last_ref[1], packed_ref.at[0], packed_ref.at[1], wide_ref, left_ref)

    @pl.when(last_ref[0] == 0)
    def _():
        join_cores(last_ref[1], near_ref, far_ref, left_ref)

    mask = block_mask(LANES, LANES)
    left = left_ref[...]
    alive = live(extent_ref)
    start = psi_ref[...].astype(f32) * alive
    image = apply_h(left, right_ref, start, mask, product_ref) * alive
    diagonal = jnp.where(iota((B, LANES), 0) == iota((B, LANES), 1) % B, 1.0, 0.0)
    tall_row = iota((W_BOND * B, LANES), 0)
    tall_row = (tall_row // (W_BOND * 8)) * 8 + tall_row % 8
    on_diagonal = jnp.where(tall_row == iota((W_BOND * B, LANES), 1) % B, 1.0, 0.0)
    picked = on_diagonal.astype(bf16) * left
    left_diag = jnp.dot(picked, mask, preferred_element_type=f32)
    precond = jnp.zeros((B, LANES), f32)
    for w in range(W_BOND):
        rows = slice(w * B, (w + 1) * B)
        right_diag = jnp.sum(right_ref[rows, :].astype(f32) * diagonal, axis=0, keepdims=True)
        precond = precond + bond_rows(left_diag, w) * right_diag
    start_ref[...] = start
    image_ref[...] = image
    precond_ref[...] = precond
    send_sums([dot_all(start, start), dot_all(start, image)], sent_ref)


def next_correction(vector, image, energy, precond, left_ref, right_ref, alive, outs):
    vector_ref, image_ref, correction_ref, lifted_ref, sent_ref, product_ref = outs
    residue = image - energy * vector
    correction = residue / jnp.maximum(precond - energy, 1.0)
    lifted = apply_h(left_ref[...], right_ref, correction, block_mask(LANES, LANES), product_ref) * alive
    vector_ref[...] = vector
    image_ref[...] = image
    correction_ref[...] = correction
    lifted_ref[...] = lifted
    send_sums(
        [
            dot_all(vector, correction),
            dot_all(correction, correction),
            dot_all(vector, vector),
            dot_all(correction, image),
            dot_all(correction, lifted),
            dot_all(vector, lifted),
            dot_all(vector, image),
        ],
        sent_ref,
    )


def one_kernel(got_ref, start_ref, raw_ref, precond_ref, left_ref, right_ref, extent_ref, *outs):
    norm, raw = take_sums(got_ref, 2)
    scale = 1.0 / jnp.sqrt(norm + epsilon)
    next_correction(
        start_ref[...] * scale,
        raw_ref[...] * scale,
        raw * scale * scale,
        precond_ref[...],
        left_ref,
        right_ref,
        live(extent_ref),
        outs,
    )


def rotated(got_ref, vector, image, correction, lifted):
    vc, cc, vv, ci, cl, vl, energy = take_sums(got_ref, 7)
    length_sq = jnp.maximum(cc - 2.0 * vc * vc + vc * vc * vv, 0.0)
    inverse = 1.0 / jnp.sqrt(length_sq + epsilon)
    direction = (correction - vc * vector) * inverse
    applied = (lifted - vc * image) * inverse
    coupling = (ci - vc * energy) * inverse
    crossed = (vl - vc * energy) * inverse
    curvature = (cl - vc * vl - vc * ci + vc * vc * energy) * inverse * inverse
    y, x = -2.0 * coupling, curvature - energy
    size = jnp.maximum(jnp.abs(x), jnp.abs(y))
    flat_case = size == 0.0
    size = jnp.where(flat_case, 1.0, size)
    y, x = y / size, jnp.where(flat_case, 1.0, x / size)
    radius = jnp.sqrt(x * x + y * y)
    large = jnp.sqrt((radius + jnp.abs(x)) / (2.0 * radius))
    small = jnp.abs(y) / (2.0 * radius * large)
    sign = jnp.where(y > 0.0, 1.0, -1.0)
    cosine = jnp.where(x >= 0.0, large, small)
    sine = sign * jnp.where(x >= 0.0, small, large)
    turned_energy = (
        cosine * cosine * energy + cosine * sine * (crossed + coupling) + sine * sine * curvature
    )
    return cosine * vector + sine * direction, cosine * image + sine * applied, turned_energy


def two_kernel(
    got_ref, v_ref, i_ref, c_ref, l_ref, precond_ref, left_ref, right_ref, extent_ref, *outs
):
    vector, image, energy = rotated(got_ref, v_ref[...], i_ref[...], c_ref[...], l_ref[...])
    next_correction(
        vector, image, energy, precond_ref[...], left_ref, right_ref, live(extent_ref), outs
    )


def last_kernel(got_ref, v_ref, i_ref, c_ref, l_ref, ground_ref):
    vector, image, energy = rotated(got_ref, v_ref[...], i_ref[...], c_ref[...], l_ref[...])
    ground_ref[0:B, :] = vector
    ground_ref[B : B + 8, :] = jnp.broadcast_to(energy, (8, LANES))


def slot_ranks(owner_grid):
    places = jnp.arange(owner_grid.shape[1])
    earlier = places[None, :] < places[:, None]
    same_owner = owner_grid[:, :, None] == owner_grid[:, None, :]
    return jnp.sum(jnp.where(same_owner & earlier[None], 1, 0), axis=2).astype(jnp.int32)


def tables(route_owner, route_sector, member):
    owner = route_owner.reshape(N_SECTOR, ROWS)
    worker = route_sector.reshape(N_SECTOR, ROWS)
    rank = slot_ranks(owner)
    slot = lax.dynamic_index_in_dim(owner * CAP + rank, member, 0, keepdims=False)
    mine = (owner == member)[:, None, :] & (rank[:, None, :] == jnp.arange(CAP)[None, :, None])
    target = jnp.sum(jnp.where(mine, worker[:, None, :] + 1, 0), axis=2)
    row = jnp.concatenate([slot, target.reshape(SLOTS)])
    return jnp.pad(row, (0, LANES - row.shape[0])).astype(bf16)


def local(
    env_in, mpo_terms, site_tensors, route_owner, route_sector, live_block_extent, psi, right_env
):
    site, sector = lax.axis_index("site"), lax.axis_index("sector")
    core, group = site % 2, sector // 8
    chain_site = group * 2 + core

    def tall(x):
        return x.reshape(SEC, W_BOND, B, B).transpose(1, 2, 0, 3).reshape(W_BOND * B, LANES)

    blocks = site_tensors.reshape(SEC, PHYS, B, B)
    table = tables(route_owner, route_sector, sector)
    tensors = jnp.concatenate(
        [
            blocks.transpose(1, 2, 0, 3).reshape(PHYS * B, LANES),
            jnp.broadcast_to(table[None], (8, LANES)),
        ],
        axis=0,
    )
    own_env = lax.dynamic_slice_in_dim(env_in, core * HALF, HALF, axis=1)
    own_env = own_env.reshape(SEC, HALF, 4, 8, B).transpose(2, 1, 3, 0, 4).reshape(HALF * B, LANES)
    near = jnp.stack([turn(tensors, step) for step in range(4)])
    near_env = turn(own_env, 0)
    far, far_env = other_core(near), other_core(near_env)
    sites = jnp.arange(N_SITE)
    places = jnp.where(sites % 2 == core, 0, 4) + (group - sites // 2) % 4
    places = jnp.pad(jnp.concatenate([places, core[None]]), (0, LANES - N_SITE - 1))
    info = jnp.concatenate([near[:, PHYS * B], far[:, PHYS * B]]).astype(jnp.int32)
    info = jnp.concatenate([info, places[None].astype(jnp.int32)])

    own_bonds = lax.dynamic_slice_in_dim(mpo_terms, core * HALF, HALF, axis=2)
    mpo = own_bonds.transpose(0, 2, 1).reshape(PHYS * HALF, 1, W_BOND, 1) * jnp.eye(8, dtype=bf16)[None, :, None, :]
    mpo = lax.optimization_barrier(mpo.reshape(PHYS * HALF * 8, W_BOND * 8))

    davidson = jnp.concatenate(
        [
            tall(right_env),
            psi.reshape(SEC, B, B).transpose(1, 0, 2).reshape(B, LANES),
            jnp.broadcast_to(jnp.repeat(live_block_extent, B)[None], (8, LANES)).astype(bf16),
        ],
        axis=0,
    )

    outbox_shape = ((SLOTS, PACK, 128), bf16)
    tall_shape = ((W_BOND * B, LANES), bf16)
    wide_scratch = pltpu.VMEM((LANES, 384), f32)
    product_scratch = pltpu.VMEM((W_BOND * B, LANES), f32)
    def step_of(i):
        return jnp.full((1,), i, jnp.int32)

    def leave(i, outbox):
        return run_collect(step_of(i), info, exchange(outbox))

    def enter(i, mine, saved):
        other = other_core(mine)
        return other, jnp.where(chain_site == i, jnp.stack([mine, other]), saved)

    def one_site(i, mine, saved):
        other, saved = enter(i, mine, saved)
        return leave(i, run_expand(step_of(i), info, mpo, near, far, mine, other)), saved

    (outbox,) = call(
        first_kernel, [info, mpo, near, far, near_env, far_env], [outbox_shape], [pltpu.VMEM(*tall_shape)]
    )
    mine, saved = leave(0, outbox), jnp.zeros((2, SEC, PACK, 128), bf16)
    other, saved = enter(1, mine, saved)
    mine, other, davidson = lax.optimization_barrier((mine, other, davidson))
    davidson = turn(davidson, 0)
    mine = leave(1, run_expand(step_of(1), info, mpo, near, far, mine, other))
    other, saved = enter(2, mine, saved)
    mine, other, davidson, saved = lax.optimization_barrier((mine, other, davidson, saved))
    mine = leave(2, run_expand(step_of(2), info, mpo, near, far, mine, other))

    def two_sites(turn_index, state):
        mine, saved = state
        for k in range(2):
            mine, saved = one_site(3 + 2 * turn_index + k, mine, saved)
        return mine, saved

    mine, saved = lax.fori_loop(0, 2, two_sites, (mine, saved))
    other, saved = enter(N_SITE - 1, mine, saved)

    right = davidson[: W_BOND * B]
    field, extent = davidson[W_BOND * B : W_BOND * B + B], davidson[W_BOND * B + B :]
    field_shape = ((B, LANES), f32)
    sums_shape = ((N_SECTOR, 1, 128), f32)
    last = jnp.stack([chain_site, core])
    left, start, raw, precond, sent = call(
        start_kernel,
        [last, saved, near_env, far_env, right, field, extent],
        [tall_shape, field_shape, field_shape, field_shape, sums_shape],
        [wide_scratch, product_scratch],
    )
    state = [start, raw]
    for step in range(DAV_ITERS):
        kernel = one_kernel if step == 0 else two_kernel
        *state, sent = call(
            kernel,
            [exchange(sent), *state, precond, left, right, extent],
            [field_shape] * 4 + [sums_shape],
            [product_scratch],
        )
    (result,) = call(last_kernel, [exchange(sent), *state], [((B + 8, LANES), f32)])
    result = turn(result, 0)
    ground = result[:B].reshape(B, SEC, B).transpose(1, 0, 2).reshape(1, SEC, B * B)
    return (ground, result[B, :1])


def solution(mesh):
    in_specs = (
        P("sector", None, None),
        P(),
        P("site", "sector", None, None),
        P("site", None, None, None),
        P("site", None, None),
        P("sector"),
        P("site", "sector", None),
        P("site", "sector", None, None),
    )
    out_specs = (P("site", "sector", None), P("site"))
    return jax.shard_map(local, mesh=mesh, in_specs=in_specs, out_specs=out_specs, check_vma=False)
```

```python
import functools

import jax
import jax.numpy as jnp
from jax import lax
from jax.experimental import pallas as pl
from jax.experimental.pallas import tpu as pltpu
from jax.sharding import PartitionSpec as P

B = 32
W_BOND = 20
HALF = W_BOND // 2
PHYS = 4
SEC = 8
DAV_ITERS = 2
CAP = 2
N_SITE = 8
N_SECTOR = 32
SLOTS = N_SECTOR * CAP
ROWS = SEC * PHYS
LANES = SEC * B
PACK = 48
COUNT_ALL = float(N_SECTOR * SEC * B * B)
epsilon = 1e-06
bf16, f32 = jnp.bfloat16, jnp.float32
BOTH = ("site", "sector")


def flat(high, low_core, group, rest):
    return (high * 2 + low_core) * N_SECTOR + group * 8 + rest


def every_device():
    return [(y, c, g, r) for y in range(4) for c in range(2) for g in range(4) for r in range(8)]


def turn(block, step):
    pairs = [(flat(y, c, g, r), flat(g, c, (y + step) % 4, r)) for y, c, g, r in every_device()]
    return lax.ppermute(block, BOTH, pairs)


def exchange(block):
    groups = [
        [flat(y, c, g, r) for y in range(4) for r in range(8)] for g in range(4) for c in range(2)
    ]
    return lax.all_to_all(block, BOTH, split_axis=0, concat_axis=0, tiled=True, axis_index_groups=groups)


def other_core(block):
    return lax.ppermute(block, "site", [(i, i ^ 1) for i in range(N_SITE)])


def iota(shape, axis):
    return lax.broadcasted_iota(jnp.int32, shape, axis)


def block_mask(rows, lanes):
    same = (iota((rows, lanes), 0) // B) == (iota((rows, lanes), 1) // B)
    return jnp.where(same, 1.0, 0.0).astype(bf16)


def spread_blocks(field, mask):
    return jnp.concatenate([field] * SEC, axis=0) * mask


def column_block():
    return (iota((8, 128), 1) % B) // 8


def lane_map(sources):
    return jnp.where(iota((128, 256), 0) == sources, 1.0, 0.0).astype(bf16)


def outward():
    lane = iota((128, 256), 1)
    inner = lane % 128
    source = ((inner // B) % 2) * B + 4 * ((inner % B) // 8) + inner % 4
    used = (inner % 8 >= 4) & ((inner < 64) == (lane < 128))
    return lane_map(jnp.where(used, source, -1))


def inward():
    lane = iota((128, 256), 1)
    inner = lane % 128
    source = (inner // B) * B + 8 * ((inner % B) // 4) + 4 + inner % 4
    used = (inner < 64) & (inner % B < 16)
    return lane_map(jnp.where(used, source + jnp.where(lane < 128, 0, 64), -1))


def relocated(tiles, matrix):
    stacked = jnp.concatenate(tiles, axis=0).astype(bf16)
    images = jnp.dot(stacked, matrix, preferred_element_type=f32)
    rows = [slice(8 * k, 8 * k + 8) for k in range(len(tiles))]
    return [(images[r, :128], images[r, 128:]) for r in rows]


def halves_to_tiles(squares, matrix):
    cb, lane = column_block(), iota((8, 128), 1)

    def chosen(step, tile):
        parts = [tile[8 * d : 8 * d + 8, :] for d in range(4)]
        picked = parts[(3 + step) % 4]
        for d in (2, 1, 0):
            picked = jnp.where(cb == d, parts[(d + step) % 4], picked)
        return picked

    extras = relocated([chosen(2, square[2]) for square in squares], matrix)
    for (first, second, third), (low, high) in zip(squares, extras):
        near = pltpu.roll(chosen(1, third), 64, 1)
        yield [
            jnp.where(repeated(), low + pltpu.roll(high, 4, 0), chosen(0, first)),
            chosen(0, second),
            chosen(1, first),
            chosen(1, second),
            jnp.where(lane < 64, chosen(0, third), near),
            jnp.where(cb < 2, chosen(2, first), pltpu.roll(chosen(2, second), 16, 1)),
        ]


def repeated():
    return (iota((8, 128), 0) < 4) & (iota((8, 128), 1) % 8 >= 4)


def tiles_to_half(tiles, extra):
    cb = column_block()
    diag = [tiles[0], tiles[1], tiles[4]]
    near = [tiles[2], tiles[3], pltpu.roll(tiles[4], 64, 1)]
    low, high = extra
    extra = jnp.where(iota((8, 128), 0) < 4, low, pltpu.roll(high, 4, 0))
    far = [tiles[5], pltpu.roll(tiles[5], 112, 1), extra]
    square = []
    for tile in range(3):
        rows = []
        for d in range(4):
            rows.append(
                jnp.where(
                    cb == d, diag[tile], jnp.where(cb == (d - 1) % 4, near[tile], far[tile])
                )
            )
        square.append(jnp.concatenate(rows, axis=0))
    return square


def moved(sources, shifts):
    quarter = iota((B, 128), 1) // B
    total = None
    for k, (source, shift) in enumerate(zip(sources, shifts)):
        shift = shift % 128
        piece = pltpu.roll(source, shift, 1) if shift else source
        total = piece if total is None else jnp.where(quarter == k, piece, total)
    return total


def write_tall(core, mine_ref, other_ref, wide_ref, tall_ref):
    first = jnp.full((PACK, 128), core, jnp.int32) == 0
    ab = iota((B, LANES), 0) // 8
    bb = (iota((B, LANES), 1) % B) // 8
    gap = (ab - bb) & 3
    spare = (gap == 0) & (iota((B, LANES), 0) % 8 < 4) & (iota((B, LANES), 1) % 8 >= 4)
    matrix = inward()
    valid = ((gap < 2) & jnp.logical_not(spare)) | ((gap == 2) & (bb < 2))
    for half in range(2):
        def part(t, rows):
            mine, other = mine_ref[t, rows, :].astype(f32), other_ref[t, rows, :].astype(f32)
            here = first[rows]
            return jnp.where(here, mine, other) if half == 0 else jnp.where(here, other, mine)

        squares = []
        extras = relocated([part(t, slice(0, 16))[:8] for t in range(SEC)], matrix)
        for t in range(SEC):
            whole = part(t, slice(0, PACK))
            square = tiles_to_half([whole[8 * i : 8 * i + 8, :] for i in range(6)], extras[t])
            squares.append(square)
            for tile in range(3):
                wide_ref[t * B : (t + 1) * B, tile * 128 : (tile + 1) * 128] = square[tile]
        turned = jnp.transpose(wide_ref[...])
        bonds = []
        for v in range(HALF):
            tile, offset = v // 4, (v % 4) * B
            straight = jnp.concatenate(
                [
                    moved(
                        [squares[4 * q + k][tile] for k in range(4)],
                        [k * B - offset for k in range(4)],
                    )
                    for q in range(2)
                ],
                axis=1,
            )
            bonds.append(jnp.where(valid, straight, turned[v * B : (v + 1) * B, :]))
        for d in range(4):
            for v in range(0, HALF, 2):
                pair = [bonds[v + k][8 * d : 8 * d + 8, :] for k in range(2)]
                start = (d * W_BOND + half * HALF + v) * 8
                tall_ref[start : start + 16, :] = jnp.concatenate(pair, axis=0).astype(bf16)


def bond_rows(tall, bond, bonds=W_BOND):
    return jnp.concatenate(
        [tall[(d * bonds + bond) * 8 : (d * bonds + bond) * 8 + 8, :] for d in range(4)], axis=0
    )


def join_cores(core, near_ref, far_ref, tall_ref):
    first = jnp.full((HALF * B, LANES), core, jnp.int32) == 0
    near, far = near_ref[...].astype(f32), far_ref[...].astype(f32)
    low, high = jnp.where(first, near, far).astype(bf16), jnp.where(first, far, near).astype(bf16)
    step = HALF * 8
    for d in range(4):
        tall_ref[2 * d * step : (2 * d + 1) * step, :] = low[d * step : (d + 1) * step]
        tall_ref[(2 * d + 1) * step : (2 * d + 2) * step, :] = high[d * step : (d + 1) * step]


def contract_rows(step, info_ref, mpo_ref, tensor_ref, far_tensor_ref, tall, out_ref):
    place = info_ref[N_SITE, step]
    near_core = jnp.full((B, LANES), place, jnp.int32) < 4
    turned = place & 3
    mask = block_mask(LANES, LANES)
    mixer, matrix = mpo_ref[...], outward()
    step = W_BOND * 8
    mixes = [
        jnp.dot(mixer, tall[d * step : (d + 1) * step, :], preferred_element_type=f32).astype(bf16)
        for d in range(4)
    ]
    for p in range(PHYS):
        mixed = jnp.concatenate(
            [mix[p * HALF * 8 : (p + 1) * HALF * 8, :] for mix in mixes], axis=0
        )
        rows = slice(p * B, (p + 1) * B)
        tensor = jnp.where(
            near_core, tensor_ref[turned, rows, :].astype(f32), far_tensor_ref[turned, rows, :].astype(f32)
        )
        right = spread_blocks(tensor.astype(bf16), mask)
        halfway = jnp.dot(mixed, right, preferred_element_type=f32)
        bonds = [bond_rows(halfway, v, HALF).astype(bf16) for v in range(HALF)]
        wide = []
        for s in range(SEC):
            source, offset = (s // 4) * 128, (s % 4) * B
            tiles = []
            for tile in range(3):
                here = [v for v in range(4 * tile, 4 * tile + 4) if v < HALF]
                tiles.append(
                    moved(
                        [bonds[v][:, source : source + 128] for v in here],
                        [(v % 4) * B - offset for v in here],
                    )
                )
            wide.append(jnp.concatenate(tiles, axis=1))
        wide = jnp.concatenate(wide, axis=0)
        blocks = lax.dot_general(right, wide, (((0,), (0,)), ((), ())), preferred_element_type=f32)
        squares = [
            [blocks[s * B : (s + 1) * B, tile * 128 : (tile + 1) * 128] for tile in range(3)]
            for s in range(SEC)
        ]
        for s, tiles in enumerate(halves_to_tiles(squares, matrix)):
            out_ref[info_ref[place, s * PHYS + p]] = jnp.concatenate(tiles, axis=0).astype(bf16)


def first_kernel(info_ref, mpo_ref, tensor_ref, far_tensor_ref, near_ref, far_ref, *rest):
    out_ref, tall_ref = rest
    join_cores(info_ref[N_SITE, N_SITE], near_ref, far_ref, tall_ref)
    contract_rows(0, info_ref, mpo_ref, tensor_ref, far_tensor_ref, tall_ref[...], out_ref)


def expand_kernel(step_ref, info_ref, mpo_ref, tensor_ref, far_tensor_ref, mine_ref, other_ref, *rest):
    out_ref, tall_ref, wide_ref = rest
    write_tall(info_ref[N_SITE, N_SITE], mine_ref, other_ref, wide_ref, tall_ref)
    contract_rows(step_ref[0], info_ref, mpo_ref, tensor_ref, far_tensor_ref, tall_ref[...], out_ref)


def collect_kernel(step_ref, info_ref, inbox_ref, out_ref, total_ref):
    place = info_ref[N_SITE, step_ref[0]]
    total_ref[...] = jnp.zeros_like(total_ref)
    def take(turn_index, carry):
        for k in range(4):
            q = turn_index * 4 + k
            t = info_ref[place, ROWS + q]

            @pl.when(t > 0)
            def _():
                total_ref[t - 1] += inbox_ref[q].astype(f32)

        return carry

    lax.fori_loop(0, SLOTS // 4, take, 0)
    out_ref[...] = total_ref[...].astype(bf16)


VMEM = pl.BlockSpec(memory_space=pltpu.VMEM)
SMEM = pl.BlockSpec(memory_space=pltpu.SMEM)
PARAMS = pltpu.CompilerParams(vmem_limit_bytes=48 << 20)


def call(kernel, ins, outs, scratch=()):
    shapes = [jax.ShapeDtypeStruct(shape, dtype) for shape, dtype in outs]
    specs = [SMEM if x.dtype == jnp.int32 else VMEM for x in ins]
    return pl.pallas_call(
        kernel,
        out_shape=shapes,
        in_specs=specs,
        out_specs=[VMEM] * len(shapes),
        scratch_shapes=list(scratch),
        compiler_params=PARAMS,
        name=getattr(kernel, "func", kernel).__name__,
    )(*ins)


def run_expand(i, info, mpo, near, far, mine, other):
    (outbox,) = call(
        expand_kernel,
        [i, info, mpo, near, far, mine, other],
        [((SLOTS, PACK, 128), bf16)],
        [pltpu.VMEM((W_BOND * B, LANES), bf16), pltpu.VMEM((LANES, 384), f32)],
    )
    return outbox


def run_collect(i, info, inbox):
    (mine,) = call(
        collect_kernel,
        [i, info, inbox],
        [((SEC, PACK, 128), bf16)],
        [pltpu.VMEM((SEC, PACK, 128), f32)],
    )
    return mine


def apply_h(left, right_ref, field, mask, product_ref):
    def parts(x):
        high = x.astype(bf16)
        return high, (x - high.astype(f32)).astype(bf16)

    high, low = parts(field)
    product = jnp.dot(left, spread_blocks(high, mask), preferred_element_type=f32)
    product = product + jnp.dot(left, spread_blocks(low, mask), preferred_element_type=f32)
    product_ref[...] = product

    def one_group(group, total):
        for k in range(5):
            w = group * 5 + k
            piece = jnp.concatenate(
                [product_ref[pl.ds((d * W_BOND + w) * 8, 8), :] for d in range(4)], axis=0
            )
            both = jnp.concatenate(parts(piece), axis=0)
            right = right_ref[pl.ds(pl.multiple_of(w * B, B), B), :]
            total = total + jnp.dot(both, spread_blocks(right, mask), preferred_element_type=f32)
        return total

    total = lax.fori_loop(0, W_BOND // 5, one_group, jnp.zeros((2 * B, LANES), f32))
    return total[:B] + total[B:]


def dot_all(former, latter):
    return jnp.sum(former * latter, axis=(0, 1), keepdims=True)


def send_sums(sums, sent_ref):
    lane = iota((1, 128), 1)
    row = jnp.zeros((1, 128), f32)
    for k, entry in enumerate(sums):
        row = jnp.where(lane == k, entry, row)
    sent_ref[...] = jnp.broadcast_to(row[None], (N_SECTOR, 1, 128))


def take_sums(got_ref, count):
    total = jnp.sum(got_ref[...], axis=0)
    return [total[:, k : k + 1] / COUNT_ALL for k in range(count)]


def live(extent_ref):
    extent = extent_ref[0:1, :].astype(jnp.int32)
    row, lane = iota((B, LANES), 0), iota((B, LANES), 1) % B
    return jnp.where((row < extent) & (lane < extent), 1.0, 0.0)


def start_kernel(last_ref, packed_ref, near_ref, far_ref, right_ref, psi_ref, extent_ref, *rest):
    left_ref, start_ref, image_ref, precond_ref, sent_ref, wide_ref, product_ref = rest

    @pl.when(last_ref[0] > 0)
    def _():
        write_tall(last_ref[1], packed_ref.at[0], packed_ref.at[1], wide_ref, left_ref)

    @pl.when(last_ref[0] == 0)
    def _():
        join_cores(last_ref[1], near_ref, far_ref, left_ref)

    mask = block_mask(LANES, LANES)
    left = left_ref[...]
    alive = live(extent_ref)
    start = psi_ref[...].astype(f32) * alive
    image = apply_h(left, right_ref, start, mask, product_ref) * alive
    diagonal = jnp.where(iota((B, LANES), 0) == iota((B, LANES), 1) % B, 1.0, 0.0)
    tall_row = iota((W_BOND * B, LANES), 0)
    tall_row = (tall_row // (W_BOND * 8)) * 8 + tall_row % 8
    on_diagonal = jnp.where(tall_row == iota((W_BOND * B, LANES), 1) % B, 1.0, 0.0)
    picked = on_diagonal.astype(bf16) * left
    left_diag = jnp.dot(picked, mask, preferred_element_type=f32)
    precond = jnp.zeros((B, LANES), f32)
    for w in range(W_BOND):
        rows = slice(w * B, (w + 1) * B)
        right_diag = jnp.sum(right_ref[rows, :].astype(f32) * diagonal, axis=0, keepdims=True)
        precond = precond + bond_rows(left_diag, w) * right_diag
    start_ref[...] = start
    image_ref[...] = image
    precond_ref[...] = precond
    send_sums([dot_all(start, start), dot_all(start, image)], sent_ref)


def next_correction(vector, image, energy, precond, left_ref, right_ref, alive, outs):
    vector_ref, image_ref, correction_ref, lifted_ref, sent_ref, product_ref = outs
    residue = image - energy * vector
    correction = residue / jnp.maximum(precond - energy, 1.0)
    lifted = apply_h(left_ref[...], right_ref, correction, block_mask(LANES, LANES), product_ref) * alive
    vector_ref[...] = vector
    image_ref[...] = image
    correction_ref[...] = correction
    lifted_ref[...] = lifted
    send_sums(
        [
            dot_all(vector, correction),
            dot_all(correction, correction),
            dot_all(vector, vector),
            dot_all(correction, image),
            dot_all(correction, lifted),
            dot_all(vector, lifted),
            dot_all(vector, image),
        ],
        sent_ref,
    )


def one_kernel(got_ref, start_ref, raw_ref, precond_ref, left_ref, right_ref, extent_ref, *outs):
    norm, raw = take_sums(got_ref, 2)
    scale = 1.0 / jnp.sqrt(norm + epsilon)
    next_correction(
        start_ref[...] * scale,
        raw_ref[...] * scale,
        raw * scale * scale,
        precond_ref[...],
        left_ref,
        right_ref,
        live(extent_ref),
        outs,
    )


def rotated(got_ref, vector, image, correction, lifted):
    vc, cc, vv, ci, cl, vl, energy = take_sums(got_ref, 7)
    length_sq = jnp.maximum(cc - 2.0 * vc * vc + vc * vc * vv, 0.0)
    inverse = 1.0 / jnp.sqrt(length_sq + epsilon)
    direction = (correction - vc * vector) * inverse
    applied = (lifted - vc * image) * inverse
    coupling = (ci - vc * energy) * inverse
    crossed = (vl - vc * energy) * inverse
    curvature = (cl - vc * vl - vc * ci + vc * vc * energy) * inverse * inverse
    y, x = -2.0 * coupling, curvature - energy
    size = jnp.maximum(jnp.abs(x), jnp.abs(y))
    flat_case = size == 0.0
    size = jnp.where(flat_case, 1.0, size)
    y, x = y / size, jnp.where(flat_case, 1.0, x / size)
    radius = jnp.sqrt(x * x + y * y)
    large = jnp.sqrt((radius + jnp.abs(x)) / (2.0 * radius))
    small = jnp.abs(y) / (2.0 * radius * large)
    sign = jnp.where(y > 0.0, 1.0, -1.0)
    cosine = jnp.where(x >= 0.0, large, small)
    sine = sign * jnp.where(x >= 0.0, small, large)
    turned_energy = (
        cosine * cosine * energy + cosine * sine * (crossed + coupling) + sine * sine * curvature
    )
    return cosine * vector + sine * direction, cosine * image + sine * applied, turned_energy


def two_kernel(
    got_ref, v_ref, i_ref, c_ref, l_ref, precond_ref, left_ref, right_ref, extent_ref, *outs
):
    vector, image, energy = rotated(got_ref, v_ref[...], i_ref[...], c_ref[...], l_ref[...])
    next_correction(
        vector, image, energy, precond_ref[...], left_ref, right_ref, live(extent_ref), outs
    )


def last_kernel(got_ref, v_ref, i_ref, c_ref, l_ref, ground_ref):
    vector, image, energy = rotated(got_ref, v_ref[...], i_ref[...], c_ref[...], l_ref[...])
    ground_ref[0:B, :] = vector
    ground_ref[B : B + 8, :] = jnp.broadcast_to(energy, (8, LANES))


def slot_ranks(owner_grid):
    places = jnp.arange(owner_grid.shape[1])
    earlier = places[None, :] < places[:, None]
    same_owner = owner_grid[:, :, None] == owner_grid[:, None, :]
    return jnp.sum(jnp.where(same_owner & earlier[None], 1, 0), axis=2).astype(jnp.int32)


def tables(route_owner, route_sector, member):
    owner = route_owner.reshape(N_SECTOR, ROWS)
    worker = route_sector.reshape(N_SECTOR, ROWS)
    rank = slot_ranks(owner)
    slot = lax.dynamic_index_in_dim(owner * CAP + rank, member, 0, keepdims=False)
    mine = (owner == member)[:, None, :] & (rank[:, None, :] == jnp.arange(CAP)[None, :, None])
    target = jnp.sum(jnp.where(mine, worker[:, None, :] + 1, 0), axis=2)
    row = jnp.concatenate([slot, target.reshape(SLOTS)])
    return jnp.pad(row, (0, LANES - row.shape[0])).astype(bf16)


def local(
    env_in, mpo_terms, site_tensors, route_owner, route_sector, live_block_extent, psi, right_env
):
    site, sector = lax.axis_index("site"), lax.axis_index("sector")
    core, group = site % 2, sector // 8
    chain_site = group * 2 + core

    def tall(x):
        return x.reshape(SEC, W_BOND, B, B).transpose(1, 2, 0, 3).reshape(W_BOND * B, LANES)

    blocks = site_tensors.reshape(SEC, PHYS, B, B)
    table = tables(route_owner, route_sector, sector)
    tensors = jnp.concatenate(
        [
            blocks.transpose(1, 2, 0, 3).reshape(PHYS * B, LANES),
            jnp.broadcast_to(table[None], (8, LANES)),
        ],
        axis=0,
    )
    own_env = lax.dynamic_slice_in_dim(env_in, core * HALF, HALF, axis=1)
    own_env = own_env.reshape(SEC, HALF, 4, 8, B).transpose(2, 1, 3, 0, 4).reshape(HALF * B, LANES)
    near = jnp.stack([turn(tensors, step) for step in range(4)])
    near_env = turn(own_env, 0)
    far, far_env = other_core(near), other_core(near_env)
    sites = jnp.arange(N_SITE)
    places = jnp.where(sites % 2 == core, 0, 4) + (group - sites // 2) % 4
    places = jnp.pad(jnp.concatenate([places, core[None]]), (0, LANES - N_SITE - 1))
    info = jnp.concatenate([near[:, PHYS * B], far[:, PHYS * B]]).astype(jnp.int32)
    info = jnp.concatenate([info, places[None].astype(jnp.int32)])

    own_bonds = lax.dynamic_slice_in_dim(mpo_terms, core * HALF, HALF, axis=2)
    mpo = own_bonds.transpose(0, 2, 1).reshape(PHYS * HALF, 1, W_BOND, 1) * jnp.eye(8, dtype=bf16)[None, :, None, :]
    mpo = lax.optimization_barrier(mpo.reshape(PHYS * HALF * 8, W_BOND * 8))

    davidson = jnp.concatenate(
        [
            tall(right_env),
            psi.reshape(SEC, B, B).transpose(1, 0, 2).reshape(B, LANES),
            jnp.broadcast_to(jnp.repeat(live_block_extent, B)[None], (8, LANES)).astype(bf16),
        ],
        axis=0,
    )

    outbox_shape = ((SLOTS, PACK, 128), bf16)
    tall_shape = ((W_BOND * B, LANES), bf16)
    wide_scratch = pltpu.VMEM((LANES, 384), f32)
    product_scratch = pltpu.VMEM((W_BOND * B, LANES), f32)
    def step_of(i):
        return jnp.full((1,), i, jnp.int32)

    def leave(i, outbox):
        return run_collect(step_of(i), info, exchange(outbox))

    def enter(i, mine, saved):
        other = other_core(mine)
        return other, jnp.where(chain_site == i, jnp.stack([mine, other]), saved)

    def one_site(i, mine, saved):
        other, saved = enter(i, mine, saved)
        return leave(i, run_expand(step_of(i), info, mpo, near, far, mine, other)), saved

    (outbox,) = call(
        first_kernel, [info, mpo, near, far, near_env, far_env], [outbox_shape], [pltpu.VMEM(*tall_shape)]
    )
    mine, saved = leave(0, outbox), jnp.zeros((2, SEC, PACK, 128), bf16)
    other, saved = enter(1, mine, saved)
    mine, other, davidson = lax.optimization_barrier((mine, other, davidson))
    davidson = turn(davidson, 0)
    mine = leave(1, run_expand(step_of(1), info, mpo, near, far, mine, other))
    other, saved = enter(2, mine, saved)
    closing = chain_site == N_SITE - 1
    mine, other, davidson, saved, closing = lax.optimization_barrier(
        (mine, other, davidson, saved, closing)
    )
    mine = leave(2, run_expand(step_of(2), info, mpo, near, far, mine, other))

    def two_sites(turn_index, state):
        mine, saved = state
        for k in range(2):
            mine, saved = one_site(3 + 2 * turn_index + k, mine, saved)
        return mine, saved

    mine, saved = lax.fori_loop(0, 2, two_sites, (mine, saved))
    other = other_core(mine)
    saved = jnp.where(closing, jnp.stack([mine, other]), saved)

    right = davidson[: W_BOND * B]
    field, extent = davidson[W_BOND * B : W_BOND * B + B], davidson[W_BOND * B + B :]
    field_shape = ((B, LANES), f32)
    sums_shape = ((N_SECTOR, 1, 128), f32)
    last = jnp.stack([chain_site, core])
    left, start, raw, precond, sent = call(
        start_kernel,
        [last, saved, near_env, far_env, right, field, extent],
        [tall_shape, field_shape, field_shape, field_shape, sums_shape],
        [wide_scratch, product_scratch],
    )
    state = [start, raw]
    for step in range(DAV_ITERS):
        kernel = one_kernel if step == 0 else two_kernel
        *state, sent = call(
            kernel,
            [exchange(sent), *state, precond, left, right, extent],
            [field_shape] * 4 + [sums_shape],
            [product_scratch],
        )
    (result,) = call(last_kernel, [exchange(sent), *state], [((B + 8, LANES), f32)])
    result = turn(result, 0)
    ground = result[:B].reshape(B, SEC, B).transpose(1, 0, 2).reshape(1, SEC, B * B)
    return (ground, result[B, :1])


def solution(mesh):
    in_specs = (
        P("sector", None, None),
        P(),
        P("site", "sector", None, None),
        P("site", None, None, None),
        P("site", None, None),
        P("sector"),
        P("site", "sector", None),
        P("site", "sector", None, None),
    )
    out_specs = (P("site", "sector", None), P("site"))
    return jax.shard_map(local, mesh=mesh, in_specs=in_specs, out_specs=out_specs, check_vma=False)
```
